32 devices in a mesh: expert: 4 (over z), dp: 8 (over y, x, core).
Axes of the slice: x: 2, y: 2, z: 4, core: 2. Of those that a mesh axis runs over, the one named last changes fastest.
Arguments:
- grad_out: bfloat16 [4096, 2048], P(('expert', 'dp')), may hold values from -1.59375 to 1.59375
- slot_token: int32 [32, 8, 8], P(('expert', 'dp')), may hold values from 0 to 127, as said below
- hidden: bfloat16 [2048, 768], P(('expert', 'dp')), may hold values from -6 to 6
- slot_weight: float32 [32, 64], P(('expert', 'dp')), may hold values from 0.05 to 0.5
- counts: int32 [32, 8], P(('expert', 'dp')), may hold values from 0 to 8, as said below
- master_weight: bfloat16 [8, 768, 2048], P('expert', 'dp')
- moment1: bfloat16 [8, 768, 2048], P('expert', 'dp')
- moment2: bfloat16 [8, 768, 2048], P('expert', 'dp'), may hold values from 0.099609375 to 2
Outputs:
- new_weight: bfloat16 [8, 768, 2048], P('expert', 'dp')
The draws below stay inside these ranges and needn't reach their ends.
Inputs may be any that keep to these rules, and one draw needn't show every extreme that they name: `slot_token`: within one device's block for one expert, the 8 slots name different tokens. `counts`: in every draw some expert has 8 live slots from every device.
All inputs are finite; a program needn't handle non-finite values.
Results may differ from the reference program's by a relative error of at most 0.0055.
Values may be sent and summed in bfloat16 or wider, within the bound.
A program may use at most 64 MiB of HBM per device.

```python
import math
import jax
import jax.numpy as jnp
from jax import lax

MODEL_WIDTH = 2048
EXPERT_HIDDEN = 768
EXPERTS_DEV = 2
TOKENS_DEV = 128
CAPACITY = 8
EXPERTS = 8
SOURCES = 32
TOKENS = 4096
SLOT_ROWS = 2048
N_EXPERT = 4
N_DP = 8


def scaled_matrices(key, amplitude):
    first_key, second_key = jax.random.split(key, 2)
    full_shape = (EXPERTS, EXPERT_HIDDEN, MODEL_WIDTH)
    row_scale = jnp.exp(jax.random.uniform(second_key, (EXPERTS, EXPERT_HIDDEN, 1), jnp.float32, 0.0, 2.3026))
    rising = jnp.exp(jnp.arange(EXPERT_HIDDEN, dtype=jnp.float32) * (1.0986123 / max(EXPERT_HIDDEN - 1, 1)))[None, :, None]
    base_value = jax.random.normal(first_key, full_shape, jnp.float32)
    return (amplitude * base_value * row_scale * rising / 4.0).astype(jnp.bfloat16)


def draw_master_weight(key, part):
    return scaled_matrices(jax.random.fold_in(key, 11), 1.0)


def draw_moment1(key, part):
    return scaled_matrices(jax.random.fold_in(key, 12), 0.1)


def draw_slot_token(key, part):
    base_token = jax.random.randint(jax.random.fold_in(key, 13), (SOURCES, EXPERTS, 1), 0, TOKENS_DEV)
    return ((base_token + jnp.arange(CAPACITY, dtype=jnp.int32)[None, None, :]) % TOKENS_DEV).astype(jnp.int32)


def draw_counts(key, part):
    first_key, second_key = jax.random.split(jax.random.fold_in(key, 14))
    hot_number = max(1, EXPERTS // 16)
    order = jax.random.permutation(second_key, EXPERTS)
    is_hot = order < hot_number
    cold = jax.random.randint(first_key, (SOURCES, N_EXPERT, EXPERTS_DEV), 0, CAPACITY // 2 + 1)
    group = jnp.arange(SOURCES, dtype=jnp.int32) // N_DP
    expert_id = group[:, None] * EXPERTS_DEV + jnp.arange(EXPERTS_DEV, dtype=jnp.int32)[None, :]
    hot_here = jnp.take(is_hot, expert_id, axis=0)[:, None, :]
    return jnp.where(hot_here, CAPACITY, cold).reshape(SOURCES, N_EXPERT * EXPERTS_DEV).astype(jnp.int32)


def block_levels(rng, extent, shards, least, high):
    loudness = 1.0
    for axis_at, shards_of in shards:
        heights = jax.random.uniform(jax.random.fold_in(jax.random.fold_in(rng, 6), axis_at), (shards_of,), jnp.float32, least / len(shards), high / len(shards))
        loudness = loudness * jnp.repeat(jnp.exp(heights), extent[axis_at] // shards_of).reshape((-1,) + (1,) * (len(extent) - 1 - axis_at))
    return loudness


def scatter_about(rng, extent, spread, limit, shards=(), kind=jnp.bfloat16):
    values = spread * jax.random.normal(rng, extent, jnp.float32)
    if shards:
        values = values * block_levels(rng, extent, shards, -0.22, 0.18)
    return jnp.clip(values, -limit, limit).astype(kind)


def setup_inputs(seed: int = 0) -> dict:
    arg_keys = jax.random.split(jax.random.key(seed), 9)
    return {
        "grad_out": scatter_about(arg_keys[0], (TOKENS, MODEL_WIDTH), 0.2, 1.59375, ((0, 32),)),
        "slot_token": draw_slot_token(jax.random.fold_in(arg_keys[8], 71), 0),
        "hidden": scatter_about(arg_keys[2], (SLOT_ROWS, EXPERT_HIDDEN), 1.0, 6.0, ((0, 32),)),
        "slot_weight": jnp.clip(0.05 + 0.45 * jax.random.uniform(arg_keys[3], (SOURCES, N_EXPERT * EXPERTS_DEV * CAPACITY), jnp.float32) ** block_levels(arg_keys[3], (SOURCES, N_EXPERT * EXPERTS_DEV * CAPACITY), ((0, 32),), -0.2, 0.2), 0.05, 0.5),
        "counts": draw_counts(jax.random.fold_in(arg_keys[8], 71), 0),
        "master_weight": draw_master_weight(jax.random.fold_in(arg_keys[8], 71), 0),
        "moment1": draw_moment1(jax.random.fold_in(arg_keys[8], 71), 0),
        "moment2": jnp.clip(jnp.exp(math.log(2.0) - 2.9996462 * jax.random.uniform(arg_keys[7], (EXPERTS, EXPERT_HIDDEN, MODEL_WIDTH), jnp.float32) ** block_levels(arg_keys[7], (EXPERTS, EXPERT_HIDDEN, MODEL_WIDTH), ((0, 4), (1, 8)), -0.2, 0.2)), 0.099609375, 2.0).astype(jnp.bfloat16),
    }


learn_rate = 0.3
decay_rate = 0.01
adam_eps = 1e-06
norm_eps = 1e-06
bias_one = 1.0 - 0.9 ** 10
bias_two = 1.0 - 0.999 ** 10

def lamb_step(weight, first, second, gradient):
    first_new = 0.9 * first + 0.1 * gradient
    second_new = 0.999 * second + 0.001 * gradient * gradient
    update = first_new / bias_one / (jnp.sqrt(second_new / bias_two) + adam_eps) + decay_rate * weight
    ratio = jnp.sqrt(jnp.sum(weight * weight)) / (jnp.sqrt(jnp.sum(update * update)) + norm_eps)
    return weight - learn_rate * ratio * update

def reference(grad_out, slot_token, hidden, slot_weight, counts, master_weight, moment1, moment2):
    hidden_all = hidden.reshape(N_EXPERT, N_DP, N_EXPERT, EXPERTS_DEV, CAPACITY, EXPERT_HIDDEN)
    weight_all = slot_weight.reshape(N_EXPERT, N_DP, N_EXPERT, EXPERTS_DEV, CAPACITY)
    count_all = counts.reshape(N_EXPERT, N_DP, N_EXPERT, EXPERTS_DEV)
    tokens_all = grad_out.reshape(N_EXPERT, N_DP, TOKENS_DEV, MODEL_WIDTH).transpose(1, 0, 2, 3)
    slots_all = slot_token.reshape(N_EXPERT, N_DP, N_EXPERT, EXPERTS_DEV, CAPACITY)
    slot_ids = jnp.arange(CAPACITY, dtype=jnp.int32)[None, :]

    def one_group(group):
        hidden_g = lax.dynamic_index_in_dim(hidden_all, group, 0, keepdims=False)
        weight_g = lax.dynamic_index_in_dim(weight_all, group, 0, keepdims=False)
        count_g = lax.dynamic_index_in_dim(count_all, group, 0, keepdims=False)
        slots_g = lax.dynamic_index_in_dim(slots_all, group, 2, keepdims=False).transpose(1, 0, 2, 3)

        def one_replica(total, inputs):
            rows_h, rows_w, rows_n, rows_s, tokens_d = inputs
            parts = []
            for j in range(EXPERTS_DEV):
                index = rows_s[:, j, :].astype(jnp.int32)
                dy = jnp.take_along_axis(tokens_d, index[:, :, None], axis=1)
                live = slot_ids < rows_n[:, j][:, None]
                mixing = jnp.where(live, rows_w[:, j, :], 0.0).astype(jnp.bfloat16)
                scaled = (mixing.astype(jnp.float32)[:, :, None] * dy.astype(jnp.float32)).astype(jnp.bfloat16)
                partial_value = jnp.dot(rows_h[:, j].reshape(-1, EXPERT_HIDDEN).T, scaled.reshape(-1, MODEL_WIDTH), preferred_element_type=jnp.float32)
                parts.append(partial_value.astype(jnp.bfloat16).astype(jnp.float32))
            return (total + jnp.stack(parts), None)
        start = jnp.zeros((EXPERTS_DEV, EXPERT_HIDDEN, MODEL_WIDTH), jnp.float32)
        gradient, _ = lax.scan(one_replica, start, (hidden_g, weight_g, count_g, slots_g, tokens_all))
        return gradient

    def one_expert(args):
        weight, first, second, gradient = args
        return lamb_step(weight.astype(jnp.float32), first.astype(jnp.float32), second.astype(jnp.float32), gradient).astype(jnp.bfloat16)

    def group_update(group):
        gradient = one_group(group)
        weight = lax.dynamic_slice_in_dim(master_weight, group * EXPERTS_DEV, EXPERTS_DEV, 0)
        first = lax.dynamic_slice_in_dim(moment1, group * EXPERTS_DEV, EXPERTS_DEV, 0)
        second = lax.dynamic_slice_in_dim(moment2, group * EXPERTS_DEV, EXPERTS_DEV, 0)
        return lax.map(one_expert, (weight, first, second, gradient))
    result = lax.map(group_update, jnp.arange(N_EXPERT, dtype=jnp.int32))
    return result.reshape(EXPERTS, EXPERT_HIDDEN, MODEL_WIDTH)
```

```python
import functools

import jax
import jax.numpy as jnp
from jax import lax
from jax.experimental import pallas as pl
from jax.experimental.pallas import tpu as pltpu
from jax.sharding import PartitionSpec as P

learn_rate = 0.3
decay_rate = 0.01
adam_eps = 1e-06
norm_eps = 1e-06
bias_one = 1.0 - 0.9**10
bias_two = 1.0 - 0.999**10


MESH = pl.DeviceIdType.MESH
LANES = 128
CHUNKS = 4


def fused_kernel(
    n_expert,
    chunks,
    token_ref,
    count_ref,
    mix_ref,
    grad_hbm,
    hidden_hbm,
    weight_hbm,
    first_hbm,
    second_hbm,
    out_hbm,
    grad,
    hidden,
    weight,
    first,
    second,
    outbuf,
    sendbuf,
    rows,
    hsend,
    hrecv,
    lhs,
    gradient,
    update,
    norms,
    load_sem,
    out_sem,
    z_send,
    z_recv,
    p_send,
    p_recv,
    h_send,
    h_recv,
    n_send,
    n_recv,
):
    e = lax.axis_index("expert")
    d = lax.axis_index("dp")
    core, x, y = d % 2, (d // 2) % 2, d // 4
    experts_here, share, width = weight.shape
    capacity = token_ref.shape[2]
    cols = width // chunks
    slots = experts_here * capacity
    local_rows = n_expert * slots
    pack = LANES // local_rows
    n_dp = hrecv.shape[0]
    half = n_expert // 2

    def member(fy, fx, fc):
        yy = 1 - y if fy else y
        xx = 1 - x if fx else x
        cc = 1 - core if fc else core
        return yy * 4 + xx * 2 + cc

    flips = [(f // 4, (f // 2) % 2, f % 2) for f in range(1, n_dp)]

    barrier = pltpu.get_barrier_semaphore()
    for step in range(1, n_expert):
        pl.semaphore_signal(barrier, inc=1, device_id=((e + step) % n_expert, d), device_id_type=MESH)
    for flip in flips:
        pl.semaphore_signal(barrier, inc=1, device_id=(e, member(*flip)), device_id_type=MESH)

    loads = [
        pltpu.make_async_copy(src, dst, load_sem.at[i])
        for i, (src, dst) in enumerate(
            [
                (grad_hbm, grad),
                (hidden_hbm, hidden),
                (weight_hbm, weight),
                (first_hbm, first),
                (second_hbm, second),
            ]
        )
    ]
    for copy in loads:
        copy.start()

    tokens = grad.shape[0]
    lane = lax.broadcasted_iota(jnp.int32, (8, tokens), 1)
    sub = lax.broadcasted_iota(jnp.int32, (8, tokens), 0)
    blocks = []
    for base in range(0, local_rows, 8):
        want = jnp.zeros((8, tokens), jnp.int32)
        for i in range(8):
            s = base + i
            want = jnp.where(sub == i, token_ref[0, s // capacity, s % capacity], want)
        blocks.append(jnp.where(want == lane, 1.0, 0.0))
    onehot = jnp.concatenate(blocks, axis=0).astype(jnp.bfloat16)
    loads[0].wait()
    for ch in range(chunks):
        picked = jnp.dot(
            onehot, grad[:, ch * cols : (ch + 1) * cols], preferred_element_type=jnp.float32
        ).astype(jnp.bfloat16)
        sendbuf[ch] = picked.reshape(n_expert, slots, cols)
    for ch in range(chunks):
        rows[ch, d, e] = sendbuf[ch, e]

    pl.semaphore_wait(barrier, n_expert - 1 + n_dp - 1)

    z_copies = []
    for ch in range(chunks):
        group = []
        for step in range(1, n_expert):
            peer = (e + step) % n_expert
            copy = pltpu.make_async_remote_copy(
                src_ref=sendbuf.at[ch, peer],
                dst_ref=rows.at[ch, d, e],
                send_sem=z_send.at[ch, step - 1],
                recv_sem=z_recv.at[ch, step - 1],
                device_id=(peer, d),
                device_id_type=MESH,
            )
            copy.start()
            group.append(copy)
        z_copies.append(group)

    slot = lax.broadcasted_iota(jnp.int32, (1, LANES), 1) % local_rows
    live = jnp.zeros((1, LANES), jnp.int32)
    for g in range(local_rows // capacity):
        live = jnp.where(slot // capacity == g, count_ref[0, g], live)
    mix = jnp.concatenate([mix_ref[...]] * pack, axis=1)
    mix = jnp.where(slot % capacity < live, mix, 0.0).astype(jnp.bfloat16).astype(jnp.float32)
    row_id = lax.broadcasted_iota(jnp.int32, (local_rows, LANES), 0)
    col_id = lax.broadcasted_iota(jnp.int32, (local_rows, LANES), 1)
    placed = jnp.where(col_id == row_id + (d % pack) * local_rows, mix, 0.0).astype(jnp.bfloat16)
    loads[1].wait()
    turned = lax.dot_general(
        hidden[...], placed, (((0,), (0,)), ((), ())), preferred_element_type=jnp.float32
    ).astype(jnp.bfloat16)
    hsend[...] = turned.reshape(n_dp, share, LANES)
    h_copies = []
    for i, flip in enumerate(flips):
        peer = member(*flip)
        copy = pltpu.make_async_remote_copy(
            src_ref=hsend.at[peer],
            dst_ref=hrecv.at[d],
            send_sem=h_send.at[i],
            recv_sem=h_recv.at[i],
            device_id=(e, peer),
            device_id_type=MESH,
        )
        copy.start()
        h_copies.append(copy)
    hrecv[d] = hsend[d]

    near_x, near_y, partner = member(0, 1, 0), member(1, 0, 0), member(0, 0, 1)
    across = member(1, 1, 0)

    def send(kind, ch, block, part, to):
        ref = rows.at[ch, block] if part is None else rows.at[ch, block, pl.ds(*part)]
        return pltpu.make_async_remote_copy(
            src_ref=ref,
            dst_ref=ref,
            send_sem=p_send.at[ch, kind],
            recv_sem=p_recv.at[ch, kind],
            device_id=(e, to),
            device_id_type=MESH,
        )

    low, high = (0, half), (half, n_expert - half)
    plane = []
    for ch in range(chunks):
        plane.append(
            dict(
                own_x=send(0, ch, d, None, near_x),
                own_y=send(1, ch, d, None, near_y),
                own_c=send(2, ch, d, None, partner),
                relay_y=send(3, ch, near_x, low, near_y),
                relay_x=send(4, ch, near_y, high, near_x),
                pass_x=send(5, ch, near_x, None, partner),
                pass_y=send(6, ch, near_y, None, partner),
                pass_low=send(7, ch, across, low, partner),
                pass_high=send(8, ch, across, high, partner),
            )
        )

    def stage_own(ch):
        for copy in z_copies[ch]:
            copy.wait_recv()
        p = plane[ch]
        for name in ("own_x", "own_y", "own_c"):
            p[name].start()

    def stage_relay(ch):
        p = plane[ch]
        p["own_x"].wait_recv()
        p["relay_y"].start()
        p["pass_x"].start()
        p["own_y"].wait_recv()
        p["relay_x"].start()
        p["pass_y"].start()

    def stage_pass(ch):
        p = plane[ch]
        p["relay_y"].wait_recv()
        p["pass_low"].start()
        p["relay_x"].wait_recv()
        p["pass_high"].start()

    def stage_lhs():
        for copy in h_copies:
            copy.wait_recv()
        kind = (lax.broadcasted_iota(jnp.int32, (share, LANES), 1) % slots) // capacity
        for q in range(n_dp // pack):
            block = hrecv[q * pack].astype(jnp.float32)
            for r in range(1, pack):
                block = block + hrecv[q * pack + r].astype(jnp.float32)
            for j in range(experts_here):
                lhs[j * share : (j + 1) * share, q * LANES : (q + 1) * LANES] = jnp.where(
                    kind == j, block, 0.0
                ).astype(jnp.bfloat16)
        for copy in loads[2:]:
            copy.wait()

    tile = 16
    zero = jnp.zeros((tile, LANES), jnp.float32)

    def fold(value):
        total = value[:, :LANES]
        for at in range(LANES, cols, LANES):
            total = total + value[:, at : at + LANES]
        return total

    sums = [(zero, zero) for _ in range(experts_here)]

    def stage_update(ch):
        p = plane[ch]
        for name in ("own_c", "pass_x", "pass_y", "pass_low", "pass_high"):
            p[name].wait_recv()
        gradient[...] = jnp.dot(
            lhs[...], rows[ch].reshape(n_dp * local_rows, cols), preferred_element_type=jnp.float32
        )
        at = slice(ch * cols, (ch + 1) * cols)
        for j in range(experts_here):

            def block(r, carry, j=j):
                here = pl.ds(pl.multiple_of(r * tile, tile), tile)
                there = pl.ds(pl.multiple_of(j * share + r * tile, tile), tile)
                g = gradient[there, :]
                w = weight[j, here, at].astype(jnp.float32)
                m = 0.9 * first[j, here, at].astype(jnp.float32) + 0.1 * g
                v = 0.999 * second[j, here, at].astype(jnp.float32) + 0.001 * g * g
                u = m / bias_one / (jnp.sqrt(v / bias_two) + adam_eps) + decay_rate * w
                update[there, at] = u
                return carry[0] + fold(w * w), carry[1] + fold(u * u)

            sums[j] = lax.fori_loop(0, share // tile, block, sums[j])

    for t in range(chunks + 3):
        if t < chunks:
            stage_own(t)
        if 0 <= t - 1 < chunks:
            stage_relay(t - 1)
        if 0 <= t - 2 < chunks:
            stage_pass(t - 2)
        if t == 2:
            stage_lhs()
        if 0 <= t - 3 < chunks:
            stage_update(t - 3)

    for j in range(experts_here):
        norms[d, j : j + 1, :] = jnp.sum(sums[j][0], axis=0, keepdims=True)
        norms[d, experts_here + j : experts_here + j + 1, :] = jnp.sum(sums[j][1], axis=0, keepdims=True)
    n_copies = []
    for i, flip in enumerate(flips):
        copy = pltpu.make_async_remote_copy(
            src_ref=norms.at[d],
            dst_ref=norms.at[d],
            send_sem=n_send.at[i],
            recv_sem=n_recv.at[i],
            device_id=(e, member(*flip)),
            device_id_type=MESH,
        )
        copy.start()
        n_copies.append(copy)
    for group in z_copies:
        for copy in group:
            copy.wait_send()
    for p in plane:
        for copy in p.values():
            copy.wait_send()
    for copy in h_copies:
        copy.wait_send()
    for copy in n_copies:
        copy.wait_recv()
    total = norms[0]
    for i in range(1, n_dp):
        total = total + norms[i]
    total = jnp.sqrt(jnp.sum(total, axis=1, keepdims=True))
    outs = []
    for j in range(experts_here):
        ratio = total[j : j + 1] / (total[experts_here + j : experts_here + j + 1] + norm_eps)
        scale = learn_rate * ratio

        def finish(r, carry, j=j, scale=scale):
            here = pl.ds(pl.multiple_of(r * tile, tile), tile)
            there = pl.ds(pl.multiple_of(j * share + r * tile, tile), tile)
            fresh = weight[j, here, :].astype(jnp.float32) - scale * update[there, :]
            outbuf[j, here, :] = fresh.astype(jnp.bfloat16)
            return carry

        lax.fori_loop(0, share // tile, finish, 0)
        copy = pltpu.make_async_copy(outbuf.at[j], out_hbm.at[j], out_sem.at[j])
        copy.start()
        outs.append(copy)
    for copy in n_copies:
        copy.wait_send()
    for copy in outs:
        copy.wait()


def fused(n_expert, n_dp, grad_out, slot_token, hidden, slot_weight, counts, master_weight, moment1, moment2):
    experts_here, share, width = master_weight.shape
    capacity = slot_token.shape[2]
    slots = experts_here * capacity
    local_rows = n_expert * slots
    cols = width // CHUNKS
    half_type = jnp.bfloat16
    dma = pltpu.SemaphoreType.DMA
    anywhere = pl.BlockSpec(memory_space=pl.ANY)
    return pl.pallas_call(
        functools.partial(fused_kernel, n_expert, CHUNKS),
        out_shape=jax.ShapeDtypeStruct(master_weight.shape, half_type),
        in_specs=[
            pl.BlockSpec(memory_space=pltpu.SMEM),
            pl.BlockSpec(memory_space=pltpu.SMEM),
            pl.BlockSpec(memory_space=pltpu.VMEM),
        ]
        + [anywhere] * 5,
        out_specs=anywhere,
        scratch_shapes=[
            pltpu.VMEM(grad_out.shape, half_type),
            pltpu.VMEM(hidden.shape, half_type),
            pltpu.VMEM(master_weight.shape, half_type),
            pltpu.VMEM(master_weight.shape, half_type),
            pltpu.VMEM(master_weight.shape, half_type),
            pltpu.VMEM(master_weight.shape, half_type),
            pltpu.VMEM((CHUNKS, n_expert, slots, cols), half_type),
            pltpu.VMEM((CHUNKS, n_dp, n_expert, slots, cols), half_type),
            pltpu.VMEM((n_dp, share, LANES), half_type),
            pltpu.VMEM((n_dp, share, LANES), half_type),
            pltpu.VMEM((experts_here * share, n_dp * local_rows), half_type),
            pltpu.VMEM((experts_here * share, cols), jnp.float32),
            pltpu.VMEM((experts_here * share, width), jnp.float32),
            pltpu.VMEM((n_dp, 2 * experts_here, LANES), jnp.float32),
            dma((5,)),
            dma((experts_here,)),
            dma((CHUNKS, n_expert - 1)),
            dma((CHUNKS, n_expert - 1)),
            dma((CHUNKS, 9)),
            dma((CHUNKS, 9)),
            dma((n_dp - 1,)),
            dma((n_dp - 1,)),
            dma((n_dp - 1,)),
            dma((n_dp - 1,)),
        ],
        compiler_params=pltpu.CompilerParams(collective_id=0, has_side_effects=True),
    )(slot_token, counts, slot_weight, grad_out, hidden, master_weight, moment1, moment2)


def choose(n_expert, n_dp, *args):
    grad_out, slot_token, hidden, _, _, master_weight, _, _ = args
    experts_here, share, width = master_weight.shape
    capacity = slot_token.shape[2]
    local_rows = hidden.shape[0]
    fewer_rows = n_dp * n_expert * capacity < hidden.shape[1]
    cube = n_dp == 2**3 and n_expert % 2 == 0
    tiles = (
        LANES % local_rows == 0
        and local_rows % 8 == 0
        and n_dp % max(1, LANES // local_rows) == 0
        and (experts_here * capacity) % 16 == 0
        and share % 16 == 0
        and width % (CHUNKS * LANES) == 0
    )
    if fewer_rows and cube and tiles:
        return fused(n_expert, n_dp, *args)
    return local(*args)


def local(grad_out, slot_token, hidden, slot_weight, counts, master_weight, moment1, moment2):
    n_expert = lax.axis_size("expert")
    experts_here = master_weight.shape[0]
    capacity = slot_token.shape[2]
    width = grad_out.shape[1]
    depth = hidden.shape[1]
    weight = master_weight.astype(jnp.float32)
    first = moment1.astype(jnp.float32)
    second = moment2.astype(jnp.float32)
    weight_sq = jnp.sum(weight * weight, axis=(1, 2))
    weight_total = lax.psum(weight_sq, "dp")
    picked = jnp.take(grad_out, slot_token.reshape(-1), axis=0).reshape(
        n_expert, experts_here * capacity, width
    )
    arrived = lax.all_to_all(picked, "expert", split_axis=0, concat_axis=0, tiled=True)
    arrived = arrived.reshape(n_expert, experts_here, capacity, width)
    slot_ids = lax.broadcasted_iota(jnp.int32, (n_expert, experts_here, capacity), 2)
    is_live = slot_ids < counts.reshape(n_expert, experts_here)[:, :, None]
    mixing = jnp.where(is_live, slot_weight.reshape(n_expert, experts_here, capacity), 0.0).astype(
        jnp.bfloat16
    )
    scaled = (mixing.astype(jnp.float32)[..., None] * arrived.astype(jnp.float32)).astype(
        jnp.bfloat16
    )
    saved = hidden.reshape(n_expert, experts_here, capacity, depth)
    shares = []
    for j in range(experts_here):
        saved_rows = saved[:, j].reshape(-1, depth)
        scaled_rows = scaled[:, j].reshape(-1, width)
        term = jnp.dot(saved_rows.T, scaled_rows, preferred_element_type=jnp.float32)
        shares.append(
            lax.psum_scatter(
                term.astype(jnp.bfloat16).astype(jnp.float32).astype(jnp.bfloat16),
                "dp",
                scatter_dimension=0,
                tiled=True,
            ).astype(jnp.float32)
        )
    gradient = jnp.stack(shares)
    first_new = 0.9 * first + 0.1 * gradient
    second_new = 0.999 * second + 0.001 * gradient * gradient
    update = (
        first_new / bias_one / (jnp.sqrt(second_new / bias_two) + adam_eps) + decay_rate * weight
    )
    update_sq = jnp.sum(update * update, axis=(1, 2))
    update_total = lax.psum(update_sq, "dp")
    trust_ratio = jnp.sqrt(weight_total) / (jnp.sqrt(update_total) + norm_eps)
    fresh = weight - learn_rate * trust_ratio[:, None, None] * update
    return fresh.astype(jnp.bfloat16)


def solution(mesh):
    placed = (
        P(("expert", "dp"), None),
        P(("expert", "dp"), None, None),
        P(("expert", "dp"), None),
        P(("expert", "dp"), None),
        P(("expert", "dp"), None),
        P("expert", "dp", None),
        P("expert", "dp", None),
        P("expert", "dp", None),
    )
    step = functools.partial(choose, mesh.shape["expert"], mesh.shape["dp"])
    return jax.shard_map(
        step, mesh=mesh, in_specs=placed, out_specs=P("expert", "dp", None), check_vma=False
    )
```

```python
import functools

import jax
import jax.numpy as jnp
from jax import lax
from jax.experimental import pallas as pl
from jax.experimental.pallas import tpu as pltpu
from jax.sharding import PartitionSpec as P

learn_rate = 0.3
decay_rate = 0.01
adam_eps = 1e-06
norm_eps = 1e-06
bias_one = 1.0 - 0.9**10
bias_two = 1.0 - 0.999**10


MESH = pl.DeviceIdType.MESH
LANES = 128
CHUNKS = 2


def mix_column(mix_ref, count_ref, local_rows, capacity):
    row = lax.broadcasted_iota(jnp.int32, (local_rows, local_rows), 0)
    col = lax.broadcasted_iota(jnp.int32, (local_rows, local_rows), 1)
    lane = lax.broadcasted_iota(jnp.int32, (1, local_rows), 1)
    live = jnp.zeros((1, local_rows), jnp.int32)
    for g in range(local_rows // capacity):
        live = jnp.where(lane // capacity == g, count_ref[0, g], live)
    mix = jnp.where(lane % capacity < live, mix_ref[...], 0.0)
    mix = mix.astype(jnp.bfloat16).astype(jnp.float32)
    return jnp.sum(jnp.where(row == col, mix, 0.0), axis=1, keepdims=True)


def fused_kernel(
    n_expert,
    chunks,
    token_ref,
    count_ref,
    mix_ref,
    grad_hbm,
    hidden_hbm,
    weight_hbm,
    first_hbm,
    second_hbm,
    out_hbm,
    scale_ref,
    grad,
    hidden,
    weight,
    first,
    second,
    sendbuf,
    rows,
    hsend,
    hrecv,
    lhs,
    gradient,
    update,
    norms,
    load_sem,
    out_sem,
    z_send,
    z_recv,
    p_send,
    p_recv,
    h_send,
    h_recv,
    n_send,
    n_recv,
):
    e = lax.axis_index("expert")
    d = lax.axis_index("dp")
    core, x, y = d % 2, (d // 2) % 2, d // 4
    experts_here, share, width = weight.shape
    capacity = token_ref.shape[2]
    cols = width // chunks
    slots = experts_here * capacity
    local_rows = n_expert * slots
    n_dp = hrecv.shape[0]
    folds = LANES // local_rows
    part = share // folds

    def member(fy, fx, fc):
        yy = 1 - y if fy else y
        xx = 1 - x if fx else x
        cc = 1 - core if fc else core
        return yy * 4 + xx * 2 + cc

    flips = [(f // 4, (f // 2) % 2, f % 2) for f in range(1, n_dp)]

    barrier = pltpu.get_barrier_semaphore()
    for step in range(1, n_expert):
        pl.semaphore_signal(barrier, inc=1, device_id=((e + step) % n_expert, d), device_id_type=MESH)
    for flip in flips:
        pl.semaphore_signal(barrier, inc=1, device_id=(e, member(*flip)), device_id_type=MESH)

    loads = [
        pltpu.make_async_copy(src, dst, load_sem.at[i])
        for i, (src, dst) in enumerate(
            [
                (hidden_hbm, hidden),
                (grad_hbm, grad),
                (weight_hbm, weight),
                (first_hbm, first),
                (second_hbm, second),
            ]
        )
    ]
    loads[0].start()
    loads[1].start()

    slot = lax.broadcasted_iota(jnp.int32, (1, LANES), 1) % local_rows
    source = (slot // slots + e) % n_expert * slots + slot % slots
    row_id = lax.broadcasted_iota(jnp.int32, (local_rows, LANES), 0)
    mix_rows = mix_column(mix_ref, count_ref, local_rows, capacity)
    placed = jnp.where(row_id == source, mix_rows, 0.0).astype(jnp.bfloat16)
    loads[0].wait()
    turned = lax.dot_general(
        hidden[...], placed, (((0,), (0,)), ((), ())), preferred_element_type=jnp.float32
    )
    turned = turned.reshape(n_dp, folds, part, LANES)
    at_lane = lax.broadcasted_iota(jnp.int32, (1, 1, LANES), 2) // local_rows
    dense = turned[:, 0]
    for f in range(1, folds):
        dense = jnp.where(at_lane == f, turned[:, f], dense)
    hsend[...] = dense.astype(jnp.bfloat16)
    hrecv[d] = hsend[d]

    tokens = grad.shape[0]
    lane = lax.broadcasted_iota(jnp.int32, (8, tokens), 1)
    sub = lax.broadcasted_iota(jnp.int32, (8, tokens), 0)
    blocks = []
    for base in range(0, local_rows, 8):
        want = jnp.zeros((8, tokens), jnp.int32)
        for i in range(8):
            s = base + i
            want = jnp.where(sub == i, token_ref[0, s // capacity, s % capacity], want)
        blocks.append(jnp.where(want == lane, 1.0, 0.0))
    onehot = jnp.concatenate(blocks, axis=0).astype(jnp.bfloat16)
    loads[1].wait()
    for copy in loads[2:]:
        copy.start()
    for ch in range(chunks):
        picked = jnp.dot(
            onehot, grad[:, ch * cols : (ch + 1) * cols], preferred_element_type=jnp.float32
        ).astype(jnp.bfloat16)
        sendbuf[ch] = picked.reshape(n_expert, slots, cols)
    for ch in range(chunks):
        rows[ch, d, 0] = sendbuf[ch, e]

    pl.semaphore_wait(barrier, n_expert - 1 + n_dp - 1)

    z_copies = []
    for ch in range(chunks):
        group = []
        for step in range(1, n_expert):
            peer = (e + step) % n_expert
            copy = pltpu.make_async_remote_copy(
                src_ref=sendbuf.at[ch, peer],
                dst_ref=rows.at[ch, d, n_expert - step],
                send_sem=z_send.at[ch, step - 1],
                recv_sem=z_recv.at[ch, step - 1],
                device_id=(peer, d),
                device_id_type=MESH,
            )
            copy.start()
            group.append(copy)
        z_copies.append(group)

    near_x, near_y, partner = member(0, 1, 0), member(1, 0, 0), member(0, 0, 1)
    across = member(1, 1, 0)

    def region(piece, block, which):
        if piece == 0:
            start, size = [(0, chunks), (0, chunks // 2), (chunks // 2, chunks - chunks // 2)][which]
            return rows.at[pl.ds(start, size), block, 0]
        others = n_expert - 1
        low = others // 2 if piece % 2 else others - others // 2
        start, size = [(1, others), (1, low), (1 + low, others - low)][which]
        return rows.at[piece - 1, block, pl.ds(start, size)]

    def send(kind, piece, block, which, to):
        ref = region(piece, block, which)
        return pltpu.make_async_remote_copy(
            src_ref=ref,
            dst_ref=ref,
            send_sem=p_send.at[piece, kind],
            recv_sem=p_recv.at[piece, kind],
            device_id=(e, to),
            device_id_type=MESH,
        )

    whole, low, high = 0, 1, 2
    plane = []
    for piece in range(chunks + 1):
        plane.append(
            dict(
                own_x=send(0, piece, d, whole, near_x),
                own_y=send(1, piece, d, whole, near_y),
                own_c=send(2, piece, d, whole, partner),
                relay_y=send(3, piece, near_x, low, near_y),
                relay_x=send(4, piece, near_y, high, near_x),
                pass_x=send(5, piece, near_x, whole, partner),
                pass_y=send(6, piece, near_y, whole, partner),
                pass_low=send(7, piece, across, low, partner),
                pass_high=send(8, piece, across, high, partner),
            )
        )

    h_copies = []
    for i, flip in enumerate(flips):
        peer = member(*flip)
        copy = pltpu.make_async_remote_copy(
            src_ref=hsend.at[peer],
            dst_ref=hrecv.at[d],
            send_sem=h_send.at[i],
            recv_sem=h_recv.at[i],
            device_id=(e, peer),
            device_id_type=MESH,
        )
        h_copies.append(copy)

    def stage_own(ch):
        if ch > 0:
            for copy in z_copies[ch - 1]:
                copy.wait_recv()
        p = plane[ch]
        for name in ("own_x", "own_y", "own_c"):
            p[name].start()
        if ch == 0:
            for copy in h_copies:
                copy.start()

    def stage_relay(ch):
        p = plane[ch]
        p["own_x"].wait_recv()
        p["relay_y"].start()
        p["pass_x"].start()
        p["own_y"].wait_recv()
        p["relay_x"].start()
        p["pass_y"].start()

    def stage_pass(ch):
        p = plane[ch]
        p["relay_y"].wait_recv()
        p["pass_low"].start()
        p["relay_x"].wait_recv()
        p["pass_high"].start()

    def stage_lhs():
        for copy in h_copies:
            copy.wait_recv()
        lane_part = lax.broadcasted_iota(jnp.int32, (part, LANES), 1) // local_rows
        kind = (lax.broadcasted_iota(jnp.int32, (part, LANES), 1) % slots) // capacity
        for q in range(n_dp // folds):
            for f in range(folds):
                block = jnp.zeros((part, LANES), jnp.float32)
                for r in range(folds):
                    piece = hrecv[q * folds + r].astype(jnp.float32)
                    if r != f:
                        piece = pltpu.roll(piece, (r - f) % folds * local_rows, 1)
                    block = jnp.where(lane_part == r, piece, block)
                for j in range(experts_here):
                    top = j * share + f * part
                    lhs[top : top + part, q * LANES : (q + 1) * LANES] = jnp.where(
                        kind == j, block, 0.0
                    ).astype(jnp.bfloat16)
        for copy in loads[2:]:
            copy.wait()

    tile = 16
    zero = jnp.zeros((tile, LANES), jnp.float32)

    def fold(value):
        total = value[:, :LANES]
        for at in range(LANES, cols, LANES):
            total = total + value[:, at : at + LANES]
        return total

    sums = [(zero, zero) for _ in range(experts_here)]
    outs = []

    def stage_update(piece):
        p = plane[piece]
        for name in ("own_c", "pass_x", "pass_y", "pass_low", "pass_high"):
            p[name].wait_recv()
        if piece == 0:
            stage_lhs()
            return
        ch = piece - 1
        gradient[...] = jnp.dot(
            lhs[...], rows[ch].reshape(n_dp * local_rows, cols), preferred_element_type=jnp.float32
        )
        at = slice(ch * cols, (ch + 1) * cols)
        for j in range(experts_here):

            def block(r, carry, j=j):
                here = pl.ds(pl.multiple_of(r * tile, tile), tile)
                there = pl.ds(pl.multiple_of(j * share + r * tile, tile), tile)
                g = gradient[there, :]
                w = weight[j, here, at].astype(jnp.float32)
                m = 0.9 * first[j, here, at].astype(jnp.float32) + 0.1 * g
                v = 0.999 * second[j, here, at].astype(jnp.float32) + 0.001 * g * g
                u = m / bias_one / (jnp.sqrt(v / bias_two) + adam_eps) + decay_rate * w
                update[there, at] = u.astype(jnp.bfloat16)
                return carry[0] + fold(w * w), carry[1] + fold(u * u)

            sums[j] = lax.fori_loop(0, share // tile, block, sums[j])
        copy = pltpu.make_async_copy(update.at[:, at], out_hbm.at[:, at], out_sem.at[ch])
        copy.start()
        outs.append(copy)

    pieces = chunks + 1
    for t in range(pieces + 3):
        if t < pieces:
            stage_own(t)
        if 0 <= t - 1 < pieces:
            stage_relay(t - 1)
        if 0 <= t - 2 < pieces:
            stage_pass(t - 2)
        if 0 <= t - 3 < pieces:
            stage_update(t - 3)

    for j in range(experts_here):
        norms[d, j : j + 1, :] = jnp.sum(sums[j][0], axis=0, keepdims=True)
        norms[d, experts_here + j : experts_here + j + 1, :] = jnp.sum(sums[j][1], axis=0, keepdims=True)
    n_copies = []
    for i, flip in enumerate(flips):
        copy = pltpu.make_async_remote_copy(
            src_ref=norms.at[d],
            dst_ref=norms.at[d],
            send_sem=n_send.at[i],
            recv_sem=n_recv.at[i],
            device_id=(e, member(*flip)),
            device_id_type=MESH,
        )
        copy.start()
        n_copies.append(copy)
    for group in z_copies:
        for copy in group:
            copy.wait_send()
    for p in plane:
        for copy in p.values():
            copy.wait_send()
    for copy in h_copies:
        copy.wait_send()
    for copy in n_copies:
        copy.wait_recv()
    total = norms[0]
    for i in range(1, n_dp):
        total = total + norms[i]
    total = jnp.sqrt(jnp.sum(total, axis=1, keepdims=True))
    for j in range(experts_here):
        ratio = total[j : j + 1] / (total[experts_here + j : experts_here + j + 1] + norm_eps)
        scale_ref[j : j + 1, :] = jnp.broadcast_to(learn_rate * ratio, (1, width))
    for copy in n_copies:
        copy.wait_send()
    for copy in outs:
        copy.wait()


def fused(n_expert, n_dp, grad_out, slot_token, hidden, slot_weight, counts, master_weight, moment1, moment2):
    experts_here, share, width = master_weight.shape
    capacity = slot_token.shape[2]
    slots = experts_here * capacity
    local_rows = n_expert * slots
    cols = width // CHUNKS
    half_type = jnp.bfloat16
    dma = pltpu.SemaphoreType.DMA
    anywhere = pl.BlockSpec(memory_space=pl.ANY)
    update, scale = pl.pallas_call(
        functools.partial(fused_kernel, n_expert, CHUNKS),
        out_shape=(
            jax.ShapeDtypeStruct((experts_here * share, width), half_type),
            jax.ShapeDtypeStruct((experts_here, width), jnp.float32),
        ),
        in_specs=[
            pl.BlockSpec(memory_space=pltpu.SMEM),
            pl.BlockSpec(memory_space=pltpu.SMEM),
            pl.BlockSpec(memory_space=pltpu.VMEM),
        ]
        + [anywhere] * 5,
        out_specs=(anywhere, pl.BlockSpec(memory_space=pltpu.VMEM)),
        scratch_shapes=[
            pltpu.VMEM(grad_out.shape, half_type),
            pltpu.VMEM(hidden.shape, half_type),
            pltpu.VMEM(master_weight.shape, half_type),
            pltpu.VMEM(master_weight.shape, half_type),
            pltpu.VMEM(master_weight.shape, half_type),
            pltpu.VMEM((CHUNKS, n_expert, slots, cols), half_type),
            pltpu.VMEM((CHUNKS, n_dp, n_expert, slots, cols), half_type),
            pltpu.VMEM((n_dp, share * local_rows // LANES, LANES), half_type),
            pltpu.VMEM((n_dp, share * local_rows // LANES, LANES), half_type),
            pltpu.VMEM((experts_here * share, n_dp * local_rows), half_type),
            pltpu.VMEM((experts_here * share, cols), jnp.float32),
            pltpu.VMEM((experts_here * share, width), half_type),
            pltpu.VMEM((n_dp, 2 * experts_here, LANES), jnp.float32),
            dma((5,)),
            dma((CHUNKS,)),
            dma((CHUNKS, n_expert - 1)),
            dma((CHUNKS, n_expert - 1)),
            dma((CHUNKS + 1, 9)),
            dma((CHUNKS + 1, 9)),
            dma((n_dp - 1,)),
            dma((n_dp - 1,)),
            dma((n_dp - 1,)),
            dma((n_dp - 1,)),
        ],
        compiler_params=pltpu.CompilerParams(collective_id=0, has_side_effects=True),
    )(slot_token, counts, slot_weight, grad_out, hidden, master_weight, moment1, moment2)
    update = update.reshape(master_weight.shape).astype(jnp.float32)
    fresh = master_weight.astype(jnp.float32) - scale[:, None, :] * update
    return fresh.astype(master_weight.dtype)


def choose(n_expert, n_dp, *args):
    grad_out, slot_token, hidden, _, _, master_weight, _, _ = args
    experts_here, share, width = master_weight.shape
    capacity = slot_token.shape[2]
    local_rows = hidden.shape[0]
    fewer_rows = n_dp * n_expert * capacity < hidden.shape[1]
    cube = n_dp == 2**3 and n_expert % 2 == 0
    tiles = (
        LANES % local_rows == 0
        and local_rows % 8 == 0
        and n_dp % max(1, LANES // local_rows) == 0
        and (experts_here * capacity) % 16 == 0
        and share % (16 * max(1, LANES // local_rows)) == 0
        and width % (CHUNKS * LANES) == 0
    )
    if fewer_rows and cube and tiles:
        return fused(n_expert, n_dp, *args)
    return local(*args)


def local(grad_out, slot_token, hidden, slot_weight, counts, master_weight, moment1, moment2):
    n_expert = lax.axis_size("expert")
    experts_here = master_weight.shape[0]
    capacity = slot_token.shape[2]
    width = grad_out.shape[1]
    depth = hidden.shape[1]
    weight = master_weight.astype(jnp.float32)
    first = moment1.astype(jnp.float32)
    second = moment2.astype(jnp.float32)
    weight_sq = jnp.sum(weight * weight, axis=(1, 2))
    weight_total = lax.psum(weight_sq, "dp")
    picked = jnp.take(grad_out, slot_token.reshape(-1), axis=0).reshape(
        n_expert, experts_here * capacity, width
    )
    arrived = lax.all_to_all(picked, "expert", split_axis=0, concat_axis=0, tiled=True)
    arrived = arrived.reshape(n_expert, experts_here, capacity, width)
    slot_ids = lax.broadcasted_iota(jnp.int32, (n_expert, experts_here, capacity), 2)
    is_live = slot_ids < counts.reshape(n_expert, experts_here)[:, :, None]
    mixing = jnp.where(is_live, slot_weight.reshape(n_expert, experts_here, capacity), 0.0).astype(
        jnp.bfloat16
    )
    scaled = (mixing.astype(jnp.float32)[..., None] * arrived.astype(jnp.float32)).astype(
        jnp.bfloat16
    )
    saved = hidden.reshape(n_expert, experts_here, capacity, depth)
    shares = []
    for j in range(experts_here):
        saved_rows = saved[:, j].reshape(-1, depth)
        scaled_rows = scaled[:, j].reshape(-1, width)
        term = jnp.dot(saved_rows.T, scaled_rows, preferred_element_type=jnp.float32)
        shares.append(
            lax.psum_scatter(
                term.astype(jnp.bfloat16).astype(jnp.float32).astype(jnp.bfloat16),
                "dp",
                scatter_dimension=0,
                tiled=True,
            ).astype(jnp.float32)
        )
    gradient = jnp.stack(shares)
    first_new = 0.9 * first + 0.1 * gradient
    second_new = 0.999 * second + 0.001 * gradient * gradient
    update = (
        first_new / bias_one / (jnp.sqrt(second_new / bias_two) + adam_eps) + decay_rate * weight
    )
    update_sq = jnp.sum(update * update, axis=(1, 2))
    update_total = lax.psum(update_sq, "dp")
    trust_ratio = jnp.sqrt(weight_total) / (jnp.sqrt(update_total) + norm_eps)
    fresh = weight - learn_rate * trust_ratio[:, None, None] * update
    return fresh.astype(jnp.bfloat16)


def solution(mesh):
    placed = (
        P(("expert", "dp"), None),
        P(("expert", "dp"), None, None),
        P(("expert", "dp"), None),
        P(("expert", "dp"), None),
        P(("expert", "dp"), None),
        P("expert", "dp", None),
        P("expert", "dp", None),
        P("expert", "dp", None),
    )
    step = functools.partial(choose, mesh.shape["expert"], mesh.shape["dp"])
    return jax.shard_map(
        step, mesh=mesh, in_specs=placed, out_specs=P("expert", "dp", None), check_vma=False
    )
```

```python
import functools

import jax
import jax.numpy as jnp
from jax import lax
from jax.experimental import pallas as pl
from jax.experimental.pallas import tpu as pltpu
from jax.sharding import PartitionSpec as P

learn_rate = 0.3
decay_rate = 0.01
adam_eps = 1e-06
norm_eps = 1e-06
bias_one = 1.0 - 0.9**10
bias_two = 1.0 - 0.999**10


MESH = pl.DeviceIdType.MESH
LANES = 128
CHUNKS = 2


def mix_column(mix_ref, count_ref, local_rows, capacity):
    row = lax.broadcasted_iota(jnp.int32, (local_rows, local_rows), 0)
    col = lax.broadcasted_iota(jnp.int32, (local_rows, local_rows), 1)
    lane = lax.broadcasted_iota(jnp.int32, (1, local_rows), 1)
    live = jnp.zeros((1, local_rows), jnp.int32)
    for g in range(local_rows // capacity):
        live = jnp.where(lane // capacity == g, count_ref[0, g], live)
    mix = jnp.where(lane % capacity < live, mix_ref[...], 0.0)
    mix = mix.astype(jnp.bfloat16).astype(jnp.float32)
    return jnp.sum(jnp.where(row == col, mix, 0.0), axis=1, keepdims=True)


def fused_kernel(
    n_expert,
    chunks,
    token_ref,
    count_ref,
    mix_ref,
    grad_hbm,
    hidden_hbm,
    weight_hbm,
    first_hbm,
    second_hbm,
    out_hbm,
    scale_ref,
    grad,
    hidden,
    weight,
    first,
    second,
    sendbuf,
    rows,
    hsend,
    hrecv,
    lhs,
    gradient,
    known_w,
    known_m,
    known_v,
    update,
    norms,
    load_sem,
    out_sem,
    z_send,
    z_recv,
    p_send,
    p_recv,
    h_send,
    h_recv,
    n_send,
    n_recv,
):
    e = lax.axis_index("expert")
    d = lax.axis_index("dp")
    core, x, y = d % 2, (d // 2) % 2, d // 4
    experts_here, share, width = weight.shape
    capacity = token_ref.shape[2]
    cols = width // chunks
    slots = experts_here * capacity
    local_rows = n_expert * slots
    n_dp = hrecv.shape[0]
    folds = LANES // local_rows
    part = share // folds

    def member(fy, fx, fc):
        yy = 1 - y if fy else y
        xx = 1 - x if fx else x
        cc = 1 - core if fc else core
        return yy * 4 + xx * 2 + cc

    flips = [(f // 4, (f // 2) % 2, f % 2) for f in range(1, n_dp)]

    barrier = pltpu.get_barrier_semaphore()
    for step in range(1, n_expert):
        pl.semaphore_signal(barrier, inc=1, device_id=((e + step) % n_expert, d), device_id_type=MESH)
    for flip in flips:
        pl.semaphore_signal(barrier, inc=1, device_id=(e, member(*flip)), device_id_type=MESH)

    loads = [
        pltpu.make_async_copy(src, dst, load_sem.at[i])
        for i, (src, dst) in enumerate(
            [
                (hidden_hbm, hidden),
                (grad_hbm, grad),
                (weight_hbm, weight),
                (first_hbm, first),
                (second_hbm, second),
            ]
        )
    ]
    loads[1].start()
    loads[0].start()

    tokens = grad.shape[0]
    lane = lax.broadcasted_iota(jnp.int32, (8, tokens), 1)
    sub = lax.broadcasted_iota(jnp.int32, (8, tokens), 0)
    blocks = []
    for base in range(0, local_rows, 8):
        want = jnp.zeros((8, tokens), jnp.int32)
        for i in range(8):
            s = base + i
            want = jnp.where(sub == i, token_ref[0, s // capacity, s % capacity], want)
        blocks.append(jnp.where(want == lane, 1.0, 0.0))
    onehot = jnp.concatenate(blocks, axis=0).astype(jnp.bfloat16)
    loads[1].wait()
    for copy in loads[2:]:
        copy.start()
    z_copies = []
    for ch in range(chunks):
        picked = jnp.dot(
            onehot, grad[:, ch * cols : (ch + 1) * cols], preferred_element_type=jnp.float32
        ).astype(jnp.bfloat16)
        sendbuf[ch] = picked.reshape(n_expert, slots, cols)
        rows[ch, d, 0] = sendbuf[ch, e]
        if ch == 0:
            pl.semaphore_wait(barrier, n_expert - 1 + n_dp - 1)
        group = []
        for step in range(1, n_expert):
            peer = (e + step) % n_expert
            copy = pltpu.make_async_remote_copy(
                src_ref=sendbuf.at[ch, peer],
                dst_ref=rows.at[ch, d, n_expert - step],
                send_sem=z_send.at[ch, step - 1],
                recv_sem=z_recv.at[ch, step - 1],
                device_id=(peer, d),
                device_id_type=MESH,
            )
            copy.start()
            group.append(copy)
        z_copies.append(group)

    near_x, near_y, partner = member(0, 1, 0), member(1, 0, 0), member(0, 0, 1)
    across = member(1, 1, 0)

    def region(piece, block, which):
        if piece == 0:
            start, size = [(0, chunks), (0, chunks // 2), (chunks // 2, chunks - chunks // 2)][which]
            return rows.at[pl.ds(start, size), block, 0]
        others = n_expert - 1
        low = others // 2 if piece % 2 else others - others // 2
        start, size = [(1, others), (1, low), (1 + low, others - low)][which]
        return rows.at[piece - 1, block, pl.ds(start, size)]

    def send(kind, piece, block, which, to):
        ref = region(piece, block, which)
        return pltpu.make_async_remote_copy(
            src_ref=ref,
            dst_ref=ref,
            send_sem=p_send.at[piece, kind],
            recv_sem=p_recv.at[piece, kind],
            device_id=(e, to),
            device_id_type=MESH,
        )

    whole, low, high = 0, 1, 2
    plane = []
    for piece in range(chunks + 1):
        plane.append(
            dict(
                own_x=send(0, piece, d, whole, near_x),
                own_y=send(1, piece, d, whole, near_y),
                own_c=send(2, piece, d, whole, partner),
                relay_y=send(3, piece, near_x, low, near_y),
                relay_x=send(4, piece, near_y, high, near_x),
                pass_x=send(5, piece, near_x, whole, partner),
                pass_y=send(6, piece, near_y, whole, partner),
                pass_low=send(7, piece, across, low, partner),
                pass_high=send(8, piece, across, high, partner),
            )
        )

    h_copies = []
    for i, flip in enumerate(flips):
        peer = member(*flip)
        copy = pltpu.make_async_remote_copy(
            src_ref=hsend.at[peer],
            dst_ref=hrecv.at[d],
            send_sem=h_send.at[i],
            recv_sem=h_recv.at[i],
            device_id=(e, peer),
            device_id_type=MESH,
        )
        h_copies.append(copy)

    def stage_hidden():
        slot = lax.broadcasted_iota(jnp.int32, (1, LANES), 1) % local_rows
        source = (slot // slots + e) % n_expert * slots + slot % slots
        row_id = lax.broadcasted_iota(jnp.int32, (local_rows, LANES), 0)
        mix_rows = mix_column(mix_ref, count_ref, local_rows, capacity)
        placed = jnp.where(row_id == source, mix_rows, 0.0).astype(jnp.bfloat16)
        loads[0].wait()
        turned = lax.dot_general(
            hidden[...], placed, (((0,), (0,)), ((), ())), preferred_element_type=jnp.float32
        )
        turned = turned.reshape(n_dp, folds, part, LANES)
        at_lane = lax.broadcasted_iota(jnp.int32, (1, 1, LANES), 2) // local_rows
        dense = turned[:, 0]
        for f in range(1, folds):
            dense = jnp.where(at_lane == f, turned[:, f], dense)
        hsend[...] = dense.astype(jnp.bfloat16)
        hrecv[d] = hsend[d]
        for copy in h_copies:
            copy.start()

    def stage_own(ch):
        if ch > 0:
            for copy in z_copies[ch - 1]:
                copy.wait_recv()
        p = plane[ch]
        for name in ("own_x", "own_y", "own_c"):
            p[name].start()
        if ch == 0:
            stage_hidden()
        if ch == 1:
            stage_known()

    def stage_relay(ch):
        p = plane[ch]
        p["own_x"].wait_recv()
        p["relay_y"].start()
        p["pass_x"].start()
        p["own_y"].wait_recv()
        p["relay_x"].start()
        p["pass_y"].start()

    def stage_pass(ch):
        p = plane[ch]
        p["relay_y"].wait_recv()
        p["pass_low"].start()
        p["relay_x"].wait_recv()
        p["pass_high"].start()

    def stage_lhs():
        for copy in h_copies:
            copy.wait_recv()
        lane_part = lax.broadcasted_iota(jnp.int32, (part, LANES), 1) // local_rows
        kind = (lax.broadcasted_iota(jnp.int32, (part, LANES), 1) % slots) // capacity
        for q in range(n_dp // folds):
            for f in range(folds):
                block = jnp.zeros((part, LANES), jnp.float32)
                for r in range(folds):
                    piece = hrecv[q * folds + r].astype(jnp.float32)
                    if r != f:
                        piece = pltpu.roll(piece, (r - f) % folds * local_rows, 1)
                    block = jnp.where(lane_part == r, piece, block)
                for j in range(experts_here):
                    top = j * share + f * part
                    lhs[top : top + part, q * LANES : (q + 1) * LANES] = jnp.where(
                        kind == j, block, 0.0
                    ).astype(jnp.bfloat16)

    tile = 16
    known_cols = cols
    zero = jnp.zeros((tile, LANES), jnp.float32)

    def fold(value):
        total = value[:, :LANES]
        for at in range(LANES, value.shape[1], LANES):
            total = total + value[:, at : at + LANES]
        return total

    weight_sums = [zero for _ in range(experts_here)]
    sums = [zero for _ in range(experts_here)]

    def stage_known():
        for copy in loads[2:]:
            copy.wait()
        for j in range(experts_here):

            def block(r, carry, j=j):
                here = pl.ds(pl.multiple_of(r * tile, tile), tile)
                there = pl.ds(pl.multiple_of(j * share + r * tile, tile), tile)
                for at in range(0, width, known_cols):
                    part_at = slice(at, at + known_cols)
                    w = weight[j, here, part_at].astype(jnp.float32)
                    known_w[there, part_at] = decay_rate * w
                    known_m[there, part_at] = (0.9 / bias_one) * first[j, here, part_at].astype(jnp.float32)
                    known_v[there, part_at] = (0.999 / bias_two) * second[j, here, part_at].astype(jnp.float32)
                    carry = carry + fold(w * w)
                return carry

            weight_sums[j] = lax.fori_loop(0, share // tile, block, weight_sums[j])

    outs = []

    def stage_update(piece):
        p = plane[piece]
        for name in ("own_c", "pass_x", "pass_y", "pass_low", "pass_high"):
            p[name].wait_recv()
        if piece == 0:
            stage_lhs()
            return
        ch = piece - 1
        gradient[...] = jnp.dot(
            lhs[...], rows[ch].reshape(n_dp * local_rows, cols), preferred_element_type=jnp.float32
        )
        at = slice(ch * cols, (ch + 1) * cols)
        for j in range(experts_here):

            def block(r, carry, j=j):
                there = pl.ds(pl.multiple_of(j * share + r * tile, tile), tile)
                g = gradient[there, :]
                m = known_m[there, at] + (0.1 / bias_one) * g
                v = known_v[there, at] + (0.001 / bias_two) * g * g
                u = m / (v * lax.rsqrt(v) + adam_eps) + known_w[there, at]
                update[there, at] = u.astype(jnp.bfloat16)
                return carry + fold(u * u)

            sums[j] = lax.fori_loop(0, share // tile, block, sums[j])
        copy = pltpu.make_async_copy(update.at[:, at], out_hbm.at[:, at], out_sem.at[ch])
        copy.start()
        outs.append(copy)

    pieces = chunks + 1
    for t in range(pieces + 3):
        if t < pieces:
            stage_own(t)
        if 0 <= t - 1 < pieces:
            stage_relay(t - 1)
        if 0 <= t - 2 < pieces:
            stage_pass(t - 2)
        if 0 <= t - 3 < pieces:
            stage_update(t - 3)

    for j in range(experts_here):
        norms[d, j : j + 1, :] = jnp.sum(weight_sums[j], axis=0, keepdims=True)
        norms[d, experts_here + j : experts_here + j + 1, :] = jnp.sum(sums[j], axis=0, keepdims=True)
    n_copies = []
    for i, flip in enumerate(flips):
        copy = pltpu.make_async_remote_copy(
            src_ref=norms.at[d],
            dst_ref=norms.at[d],
            send_sem=n_send.at[i],
            recv_sem=n_recv.at[i],
            device_id=(e, member(*flip)),
            device_id_type=MESH,
        )
        copy.start()
        n_copies.append(copy)
    for group in z_copies:
        for copy in group:
            copy.wait_send()
    for p in plane:
        for copy in p.values():
            copy.wait_send()
    for copy in h_copies:
        copy.wait_send()
    for copy in n_copies:
        copy.wait_recv()
    total = norms[0]
    for i in range(1, n_dp):
        total = total + norms[i]
    total = jnp.sqrt(jnp.sum(total, axis=1, keepdims=True))
    for j in range(experts_here):
        ratio = total[j : j + 1] / (total[experts_here + j : experts_here + j + 1] + norm_eps)
        scale_ref[j : j + 1, :] = jnp.broadcast_to(learn_rate * ratio, (1, width))
    for copy in n_copies:
        copy.wait_send()
    for copy in outs:
        copy.wait()


def fused(n_expert, n_dp, grad_out, slot_token, hidden, slot_weight, counts, master_weight, moment1, moment2):
    experts_here, share, width = master_weight.shape
    capacity = slot_token.shape[2]
    slots = experts_here * capacity
    local_rows = n_expert * slots
    cols = width // CHUNKS
    half_type = jnp.bfloat16
    dma = pltpu.SemaphoreType.DMA
    anywhere = pl.BlockSpec(memory_space=pl.ANY)
    update, scale = pl.pallas_call(
        functools.partial(fused_kernel, n_expert, CHUNKS),
        out_shape=(
            jax.ShapeDtypeStruct((experts_here * share, width), half_type),
            jax.ShapeDtypeStruct((experts_here, width), jnp.float32),
        ),
        in_specs=[
            pl.BlockSpec(memory_space=pltpu.SMEM),
            pl.BlockSpec(memory_space=pltpu.SMEM),
            pl.BlockSpec(memory_space=pltpu.VMEM),
        ]
        + [anywhere] * 5,
        out_specs=(anywhere, pl.BlockSpec(memory_space=pltpu.VMEM)),
        scratch_shapes=[
            pltpu.VMEM(grad_out.shape, half_type),
            pltpu.VMEM(hidden.shape, half_type),
            pltpu.VMEM(master_weight.shape, half_type),
            pltpu.VMEM(master_weight.shape, half_type),
            pltpu.VMEM(master_weight.shape, half_type),
            pltpu.VMEM((CHUNKS, n_expert, slots, cols), half_type),
            pltpu.VMEM((CHUNKS, n_dp, n_expert, slots, cols), half_type),
            pltpu.VMEM((n_dp, share * local_rows // LANES, LANES), half_type),
            pltpu.VMEM((n_dp, share * local_rows // LANES, LANES), half_type),
            pltpu.VMEM((experts_here * share, n_dp * local_rows), half_type),
            pltpu.VMEM((experts_here * share, cols), jnp.float32),
            pltpu.VMEM((experts_here * share, width), jnp.float32),
            pltpu.VMEM((experts_here * share, width), jnp.float32),
            pltpu.VMEM((experts_here * share, width), jnp.float32),
            pltpu.VMEM((experts_here * share, width), half_type),
            pltpu.VMEM((n_dp, 2 * experts_here, LANES), jnp.float32),
            dma((5,)),
            dma((CHUNKS,)),
            dma((CHUNKS, n_expert - 1)),
            dma((CHUNKS, n_expert - 1)),
            dma((CHUNKS + 1, 9)),
            dma((CHUNKS + 1, 9)),
            dma((n_dp - 1,)),
            dma((n_dp - 1,)),
            dma((n_dp - 1,)),
            dma((n_dp - 1,)),
        ],
        compiler_params=pltpu.CompilerParams(collective_id=0, has_side_effects=True),
    )(slot_token, counts, slot_weight, grad_out, hidden, master_weight, moment1, moment2)
    update = update.reshape(master_weight.shape).astype(jnp.float32)
    fresh = master_weight.astype(jnp.float32) - scale[:, None, :] * update
    return fresh.astype(master_weight.dtype)


def choose(n_expert, n_dp, *args):
    grad_out, slot_token, hidden, _, _, master_weight, _, _ = args
    experts_here, share, width = master_weight.shape
    capacity = slot_token.shape[2]
    local_rows = hidden.shape[0]
    fewer_rows = n_dp * n_expert * capacity < hidden.shape[1]
    cube = n_dp == 2**3 and n_expert % 2 == 0
    tiles = (
        LANES % local_rows == 0
        and local_rows % 8 == 0
        and n_dp % max(1, LANES // local_rows) == 0
        and (experts_here * capacity) % 16 == 0
        and share % (16 * max(1, LANES // local_rows)) == 0
        and width % (CHUNKS * LANES) == 0
    )
    if fewer_rows and cube and tiles:
        return fused(n_expert, n_dp, *args)
    return local(*args)


def local(grad_out, slot_token, hidden, slot_weight, counts, master_weight, moment1, moment2):
    n_expert = lax.axis_size("expert")
    experts_here = master_weight.shape[0]
    capacity = slot_token.shape[2]
    width = grad_out.shape[1]
    depth = hidden.shape[1]
    weight = master_weight.astype(jnp.float32)
    first = moment1.astype(jnp.float32)
    second = moment2.astype(jnp.float32)
    weight_sq = jnp.sum(weight * weight, axis=(1, 2))
    weight_total = lax.psum(weight_sq, "dp")
    picked = jnp.take(grad_out, slot_token.reshape(-1), axis=0).reshape(
        n_expert, experts_here * capacity, width
    )
    arrived = lax.all_to_all(picked, "expert", split_axis=0, concat_axis=0, tiled=True)
    arrived = arrived.reshape(n_expert, experts_here, capacity, width)
    slot_ids = lax.broadcasted_iota(jnp.int32, (n_expert, experts_here, capacity), 2)
    is_live = slot_ids < counts.reshape(n_expert, experts_here)[:, :, None]
    mixing = jnp.where(is_live, slot_weight.reshape(n_expert, experts_here, capacity), 0.0).astype(
        jnp.bfloat16
    )
    scaled = (mixing.astype(jnp.float32)[..., None] * arrived.astype(jnp.float32)).astype(
        jnp.bfloat16
    )
    saved = hidden.reshape(n_expert, experts_here, capacity, depth)
    shares = []
    for j in range(experts_here):
        saved_rows = saved[:, j].reshape(-1, depth)
        scaled_rows = scaled[:, j].reshape(-1, width)
        term = jnp.dot(saved_rows.T, scaled_rows, preferred_element_type=jnp.float32)
        shares.append(
            lax.psum_scatter(
                term.astype(jnp.bfloat16).astype(jnp.float32).astype(jnp.bfloat16),
                "dp",
                scatter_dimension=0,
                tiled=True,
            ).astype(jnp.float32)
        )
    gradient = jnp.stack(shares)
    first_new = 0.9 * first + 0.1 * gradient
    second_new = 0.999 * second + 0.001 * gradient * gradient
    update = (
        first_new / bias_one / (jnp.sqrt(second_new / bias_two) + adam_eps) + decay_rate * weight
    )
    update_sq = jnp.sum(update * update, axis=(1, 2))
    update_total = lax.psum(update_sq, "dp")
    trust_ratio = jnp.sqrt(weight_total) / (jnp.sqrt(update_total) + norm_eps)
    fresh = weight - learn_rate * trust_ratio[:, None, None] * update
    return fresh.astype(jnp.bfloat16)


def solution(mesh):
    placed = (
        P(("expert", "dp"), None),
        P(("expert", "dp"), None, None),
        P(("expert", "dp"), None),
        P(("expert", "dp"), None),
        P(("expert", "dp"), None),
        P("expert", "dp", None),
        P("expert", "dp", None),
        P("expert", "dp", None),
    )
    step = functools.partial(choose, mesh.shape["expert"], mesh.shape["dp"])
    return jax.shard_map(
        step, mesh=mesh, in_specs=placed, out_specs=P("expert", "dp", None), check_vma=False
    )
```

```python
import functools

import jax
import jax.numpy as jnp
from jax import lax
from jax.experimental import pallas as pl
from jax.experimental.pallas import tpu as pltpu
from jax.sharding import PartitionSpec as P

learn_rate = 0.3
decay_rate = 0.01
adam_eps = 1e-06
norm_eps = 1e-06
bias_one = 1.0 - 0.9**10
bias_two = 1.0 - 0.999**10


MESH = pl.DeviceIdType.MESH
LANES = 128
CHUNKS = 2


def mix_column(mix_ref, count_ref, local_rows, capacity):
    row = lax.broadcasted_iota(jnp.int32, (local_rows, local_rows), 0)
    col = lax.broadcasted_iota(jnp.int32, (local_rows, local_rows), 1)
    lane = lax.broadcasted_iota(jnp.int32, (1, local_rows), 1)
    live = jnp.zeros((1, local_rows), jnp.int32)
    for g in range(local_rows // capacity):
        live = jnp.where(lane // capacity == g, count_ref[0, g], live)
    mix = jnp.where(lane % capacity < live, mix_ref[...], 0.0)
    mix = mix.astype(jnp.bfloat16).astype(jnp.float32)
    return jnp.sum(jnp.where(row == col, mix, 0.0), axis=1, keepdims=True)


def fused_kernel(
    n_expert,
    chunks,
    token_hbm,
    count_hbm,
    mix_hbm,
    grad_hbm,
    hidden_hbm,
    weight_hbm,
    first_hbm,
    second_hbm,
    out_hbm,
    scale_ref,
    token_ref,
    count_ref,
    mix_ref,
    grad,
    hidden,
    weight,
    first,
    second,
    sendbuf,
    rows,
    hsend,
    hrecv,
    lhs,
    gradient,
    known_w,
    known_m,
    known_v,
    update,
    norms,
    load_sem,
    out_sem,
    z_send,
    z_recv,
    p_send,
    p_recv,
    h_send,
    h_recv,
    n_send,
    n_recv,
):
    e = lax.axis_index("expert")
    d = lax.axis_index("dp")
    core, x, y = d % 2, (d // 2) % 2, d // 4
    experts_here, share, width = weight.shape
    capacity = token_ref.shape[2]
    cols = width // chunks
    slots = experts_here * capacity
    local_rows = n_expert * slots
    n_dp = hrecv.shape[0]
    folds = LANES // local_rows
    part = share // folds

    def member(fy, fx, fc):
        yy = 1 - y if fy else y
        xx = 1 - x if fx else x
        cc = 1 - core if fc else core
        return yy * 4 + xx * 2 + cc

    flips = [(f // 4, (f // 2) % 2, f % 2) for f in range(1, n_dp)]

    barrier = pltpu.get_barrier_semaphore()
    for step in range(1, n_expert):
        pl.semaphore_signal(barrier, inc=1, device_id=((e + step) % n_expert, d), device_id_type=MESH)
    for flip in flips:
        pl.semaphore_signal(barrier, inc=1, device_id=(e, member(*flip)), device_id_type=MESH)

    loads = [
        pltpu.make_async_copy(src, dst, load_sem.at[i])
        for i, (src, dst) in enumerate(
            [
                (hidden_hbm, hidden),
                (grad_hbm, grad),
                (weight_hbm, weight),
                (first_hbm, first),
                (second_hbm, second),
                (count_hbm, count_ref),
                (mix_hbm, mix_ref),
                (token_hbm, token_ref),
            ]
        )
    ]
    for i in (7, 1, 0, 5, 6):
        loads[i].start()

    tokens = grad.shape[0]
    lane = lax.broadcasted_iota(jnp.int32, (8, tokens), 1)
    sub = lax.broadcasted_iota(jnp.int32, (8, tokens), 0)
    loads[7].wait()
    blocks = []
    for base in range(0, local_rows, 8):
        want = jnp.zeros((8, tokens), jnp.int32)
        for i in range(8):
            s = base + i
            want = jnp.where(sub == i, token_ref[0, s // capacity, s % capacity], want)
        blocks.append(jnp.where(want == lane, 1.0, 0.0))
    onehot = jnp.concatenate(blocks, axis=0).astype(jnp.bfloat16)
    loads[1].wait()
    for copy in loads[2:5]:
        copy.start()
    z_copies = []
    for ch in range(chunks):
        picked = jnp.dot(
            onehot, grad[:, ch * cols : (ch + 1) * cols], preferred_element_type=jnp.float32
        ).astype(jnp.bfloat16)
        sendbuf[ch] = picked.reshape(n_expert, slots, cols)
        rows[ch, d, 0] = sendbuf[ch, e]
        if ch == 0:
            pl.semaphore_wait(barrier, n_expert - 1 + n_dp - 1)
        group = []
        for step in range(1, n_expert):
            peer = (e + step) % n_expert
            copy = pltpu.make_async_remote_copy(
                src_ref=sendbuf.at[ch, peer],
                dst_ref=rows.at[ch, d, n_expert - step],
                send_sem=z_send.at[ch, step - 1],
                recv_sem=z_recv.at[ch, step - 1],
                device_id=(peer, d),
                device_id_type=MESH,
            )
            copy.start()
            group.append(copy)
        z_copies.append(group)

    near_x, near_y, partner = member(0, 1, 0), member(1, 0, 0), member(0, 0, 1)
    across = member(1, 1, 0)

    def region(piece, block, which):
        if piece == 0:
            start, size = [(0, chunks), (0, chunks // 2), (chunks // 2, chunks - chunks // 2)][which]
            return rows.at[pl.ds(start, size), block, 0]
        others = n_expert - 1
        low = others // 2 if piece % 2 else others - others // 2
        start, size = [(1, others), (1, low), (1 + low, others - low)][which]
        return rows.at[piece - 1, block, pl.ds(start, size)]

    def send(kind, piece, block, which, to):
        ref = region(piece, block, which)
        return pltpu.make_async_remote_copy(
            src_ref=ref,
            dst_ref=ref,
            send_sem=p_send.at[piece, kind],
            recv_sem=p_recv.at[piece, kind],
            device_id=(e, to),
            device_id_type=MESH,
        )

    whole, low, high = 0, 1, 2
    plane = []
    for piece in range(chunks + 1):
        plane.append(
            dict(
                own_x=send(0, piece, d, whole, near_x),
                own_y=send(1, piece, d, whole, near_y),
                own_c=send(2, piece, d, whole, partner),
                relay_y=send(3, piece, near_x, low, near_y),
                relay_x=send(4, piece, near_y, high, near_x),
                pass_x=send(5, piece, near_x, whole, partner),
                pass_y=send(6, piece, near_y, whole, partner),
                pass_low=send(7, piece, across, low, partner),
                pass_high=send(8, piece, across, high, partner),
            )
        )

    h_copies = []
    for i, flip in enumerate(flips):
        peer = member(*flip)
        copy = pltpu.make_async_remote_copy(
            src_ref=hsend.at[peer],
            dst_ref=hrecv.at[d],
            send_sem=h_send.at[i],
            recv_sem=h_recv.at[i],
            device_id=(e, peer),
            device_id_type=MESH,
        )
        h_copies.append(copy)

    def stage_hidden():
        slot = lax.broadcasted_iota(jnp.int32, (1, LANES), 1) % local_rows
        source = (slot // slots + e) % n_expert * slots + slot % slots
        row_id = lax.broadcasted_iota(jnp.int32, (local_rows, LANES), 0)
        loads[5].wait()
        loads[6].wait()
        mix_rows = mix_column(mix_ref, count_ref, local_rows, capacity)
        placed = jnp.where(row_id == source, mix_rows, 0.0).astype(jnp.bfloat16)
        loads[0].wait()
        turned = lax.dot_general(
            hidden[...], placed, (((0,), (0,)), ((), ())), preferred_element_type=jnp.float32
        )
        turned = turned.reshape(n_dp, folds, part, LANES)
        at_lane = lax.broadcasted_iota(jnp.int32, (1, 1, LANES), 2) // local_rows
        dense = turned[:, 0]
        for f in range(1, folds):
            dense = jnp.where(at_lane == f, turned[:, f], dense)
        hsend[...] = dense.astype(jnp.bfloat16)
        hrecv[d] = hsend[d]
        for copy in h_copies:
            copy.start()

    def stage_own(ch):
        if ch > 0:
            for copy in z_copies[ch - 1]:
                copy.wait_recv()
        p = plane[ch]
        for name in ("own_x", "own_y", "own_c"):
            p[name].start()
        if ch == 0:
            stage_hidden()
        if ch == 1:
            stage_known()

    def stage_relay(ch):
        p = plane[ch]
        p["own_x"].wait_recv()
        p["relay_y"].start()
        p["pass_x"].start()
        p["own_y"].wait_recv()
        p["relay_x"].start()
        p["pass_y"].start()

    def stage_pass(ch):
        p = plane[ch]
        p["relay_y"].wait_recv()
        p["pass_low"].start()
        p["relay_x"].wait_recv()
        p["pass_high"].start()

    def stage_lhs():
        for copy in h_copies:
            copy.wait_recv()
        lane_part = lax.broadcasted_iota(jnp.int32, (part, LANES), 1) // local_rows
        kind = (lax.broadcasted_iota(jnp.int32, (part, LANES), 1) % slots) // capacity
        for q in range(n_dp // folds):
            for f in range(folds):
                block = jnp.zeros((part, LANES), jnp.float32)
                for r in range(folds):
                    piece = hrecv[q * folds + r].astype(jnp.float32)
                    if r != f:
                        piece = pltpu.roll(piece, (r - f) % folds * local_rows, 1)
                    block = jnp.where(lane_part == r, piece, block)
                for j in range(experts_here):
                    top = j * share + f * part
                    lhs[top : top + part, q * LANES : (q + 1) * LANES] = jnp.where(
                        kind == j, block, 0.0
                    ).astype(jnp.bfloat16)

    tile = 16
    known_cols = cols
    zero = jnp.zeros((tile, LANES), jnp.float32)

    def fold(value):
        total = value[:, :LANES]
        for at in range(LANES, value.shape[1], LANES):
            total = total + value[:, at : at + LANES]
        return total

    weight_sums = [zero for _ in range(experts_here)]
    sums = [zero for _ in range(experts_here)]

    def stage_known():
        for copy in loads[2:5]:
            copy.wait()
        for j in range(experts_here):

            def block(r, carry, j=j):
                here = pl.ds(pl.multiple_of(r * tile, tile), tile)
                there = pl.ds(pl.multiple_of(j * share + r * tile, tile), tile)
                for at in range(0, width, known_cols):
                    part_at = slice(at, at + known_cols)
                    w = weight[j, here, part_at].astype(jnp.float32)
                    known_w[there, part_at] = decay_rate * w
                    known_m[there, part_at] = (0.9 / bias_one) * first[j, here, part_at].astype(jnp.float32)
                    known_v[there, part_at] = (0.999 / bias_two) * second[j, here, part_at].astype(jnp.float32)
                    carry = carry + fold(w * w)
                return carry

            weight_sums[j] = lax.fori_loop(0, share // tile, block, weight_sums[j])

    outs = []

    def stage_update(piece):
        p = plane[piece]
        for name in ("own_c", "pass_x", "pass_y", "pass_low", "pass_high"):
            p[name].wait_recv()
        if piece == 0:
            stage_lhs()
            return
        ch = piece - 1
        gradient[...] = jnp.dot(
            lhs[...], rows[ch].reshape(n_dp * local_rows, cols), preferred_element_type=jnp.float32
        )
        at = slice(ch * cols, (ch + 1) * cols)
        for j in range(experts_here):

            def block(r, carry, j=j):
                there = pl.ds(pl.multiple_of(j * share + r * tile, tile), tile)
                g = gradient[there, :]
                m = known_m[there, at] + (0.1 / bias_one) * g
                v = known_v[there, at] + (0.001 / bias_two) * g * g
                u = m / (v * lax.rsqrt(v) + adam_eps) + known_w[there, at]
                update[there, at] = u.astype(jnp.bfloat16)
                return carry + fold(u * u)

            sums[j] = lax.fori_loop(0, share // tile, block, sums[j])
        copy = pltpu.make_async_copy(update.at[:, at], out_hbm.at[:, at], out_sem.at[ch])
        copy.start()
        outs.append(copy)

    pieces = chunks + 1
    for t in range(pieces + 3):
        if t < pieces:
            stage_own(t)
        if 0 <= t - 1 < pieces:
            stage_relay(t - 1)
        if 0 <= t - 2 < pieces:
            stage_pass(t - 2)
        if 0 <= t - 3 < pieces:
            stage_update(t - 3)

    for j in range(experts_here):
        norms[d, j : j + 1, :] = jnp.sum(weight_sums[j], axis=0, keepdims=True)
        norms[d, experts_here + j : experts_here + j + 1, :] = jnp.sum(sums[j], axis=0, keepdims=True)
    n_copies = []
    for i, flip in enumerate(flips):
        copy = pltpu.make_async_remote_copy(
            src_ref=norms.at[d],
            dst_ref=norms.at[d],
            send_sem=n_send.at[i],
            recv_sem=n_recv.at[i],
            device_id=(e, member(*flip)),
            device_id_type=MESH,
        )
        copy.start()
        n_copies.append(copy)
    for group in z_copies:
        for copy in group:
            copy.wait_send()
    for p in plane:
        for copy in p.values():
            copy.wait_send()
    for copy in h_copies:
        copy.wait_send()
    for copy in n_copies:
        copy.wait_recv()
    total = norms[0]
    for i in range(1, n_dp):
        total = total + norms[i]
    total = jnp.sqrt(jnp.sum(total, axis=1, keepdims=True))
    for j in range(experts_here):
        ratio = total[j : j + 1] / (total[experts_here + j : experts_here + j + 1] + norm_eps)
        scale_ref[j : j + 1, :] = jnp.broadcast_to(learn_rate * ratio, (1, width))
    for copy in n_copies:
        copy.wait_send()
    for copy in outs:
        copy.wait()


def fused(n_expert, n_dp, grad_out, slot_token, hidden, slot_weight, counts, master_weight, moment1, moment2):
    experts_here, share, width = master_weight.shape
    capacity = slot_token.shape[2]
    slots = experts_here * capacity
    local_rows = n_expert * slots
    cols = width // CHUNKS
    half_type = jnp.bfloat16
    dma = pltpu.SemaphoreType.DMA
    anywhere = pl.BlockSpec(memory_space=pl.ANY)
    update, scale = pl.pallas_call(
        functools.partial(fused_kernel, n_expert, CHUNKS),
        out_shape=(
            jax.ShapeDtypeStruct((experts_here * share, width), half_type),
            jax.ShapeDtypeStruct((experts_here, width), jnp.float32),
        ),
        in_specs=[pl.BlockSpec(memory_space=pltpu.HBM)] * 8,
        out_specs=(anywhere, pl.BlockSpec(memory_space=pltpu.VMEM)),
        scratch_shapes=[
            pltpu.SMEM(slot_token.shape, slot_token.dtype),
            pltpu.SMEM(counts.shape, counts.dtype),
            pltpu.VMEM(slot_weight.shape, slot_weight.dtype),
            pltpu.VMEM(grad_out.shape, half_type),
            pltpu.VMEM(hidden.shape, half_type),
            pltpu.VMEM(master_weight.shape, half_type),
            pltpu.VMEM(master_weight.shape, half_type),
            pltpu.VMEM(master_weight.shape, half_type),
            pltpu.VMEM((CHUNKS, n_expert, slots, cols), half_type),
            pltpu.VMEM((CHUNKS, n_dp, n_expert, slots, cols), half_type),
            pltpu.VMEM((n_dp, share * local_rows // LANES, LANES), half_type),
            pltpu.VMEM((n_dp, share * local_rows // LANES, LANES), half_type),
            pltpu.VMEM((experts_here * share, n_dp * local_rows), half_type),
            pltpu.VMEM((experts_here * share, cols), jnp.float32),
            pltpu.VMEM((experts_here * share, width), jnp.float32),
            pltpu.VMEM((experts_here * share, width), jnp.float32),
            pltpu.VMEM((experts_here * share, width), jnp.float32),
            pltpu.VMEM((experts_here * share, width), half_type),
            pltpu.VMEM((n_dp, 2 * experts_here, LANES), jnp.float32),
            dma((8,)),
            dma((CHUNKS,)),
            dma((CHUNKS, n_expert - 1)),
            dma((CHUNKS, n_expert - 1)),
            dma((CHUNKS + 1, 9)),
            dma((CHUNKS + 1, 9)),
            dma((n_dp - 1,)),
            dma((n_dp - 1,)),
            dma((n_dp - 1,)),
            dma((n_dp - 1,)),
        ],
        compiler_params=pltpu.CompilerParams(collective_id=0, has_side_effects=True, vmem_limit_bytes=32 * 2**20),
    )(slot_token, counts, slot_weight, grad_out, hidden, master_weight, moment1, moment2)
    update = update.reshape(master_weight.shape).astype(jnp.float32)
    fresh = master_weight.astype(jnp.float32) - scale[:, None, :] * update
    return fresh.astype(master_weight.dtype)


def choose(n_expert, n_dp, *args):
    grad_out, slot_token, hidden, _, _, master_weight, _, _ = args
    experts_here, share, width = master_weight.shape
    capacity = slot_token.shape[2]
    local_rows = hidden.shape[0]
    fewer_rows = n_dp * n_expert * capacity < hidden.shape[1]
    cube = n_dp == 2**3 and n_expert % 2 == 0
    tiles = (
        LANES % local_rows == 0
        and local_rows % 8 == 0
        and n_dp % max(1, LANES // local_rows) == 0
        and (experts_here * capacity) % 16 == 0
        and share % (16 * max(1, LANES // local_rows)) == 0
        and width % (CHUNKS * LANES) == 0
    )
    if fewer_rows and cube and tiles:
        return fused(n_expert, n_dp, *args)
    return local(*args)


def local(grad_out, slot_token, hidden, slot_weight, counts, master_weight, moment1, moment2):
    n_expert = lax.axis_size("expert")
    experts_here = master_weight.shape[0]
    capacity = slot_token.shape[2]
    width = grad_out.shape[1]
    depth = hidden.shape[1]
    weight = master_weight.astype(jnp.float32)
    first = moment1.astype(jnp.float32)
    second = moment2.astype(jnp.float32)
    weight_sq = jnp.sum(weight * weight, axis=(1, 2))
    weight_total = lax.psum(weight_sq, "dp")
    picked = jnp.take(grad_out, slot_token.reshape(-1), axis=0).reshape(
        n_expert, experts_here * capacity, width
    )
    arrived = lax.all_to_all(picked, "expert", split_axis=0, concat_axis=0, tiled=True)
    arrived = arrived.reshape(n_expert, experts_here, capacity, width)
    slot_ids = lax.broadcasted_iota(jnp.int32, (n_expert, experts_here, capacity), 2)
    is_live = slot_ids < counts.reshape(n_expert, experts_here)[:, :, None]
    mixing = jnp.where(is_live, slot_weight.reshape(n_expert, experts_here, capacity), 0.0).astype(
        jnp.bfloat16
    )
    scaled = (mixing.astype(jnp.float32)[..., None] * arrived.astype(jnp.float32)).astype(
        jnp.bfloat16
    )
    saved = hidden.reshape(n_expert, experts_here, capacity, depth)
    shares = []
    for j in range(experts_here):
        saved_rows = saved[:, j].reshape(-1, depth)
        scaled_rows = scaled[:, j].reshape(-1, width)
        term = jnp.dot(saved_rows.T, scaled_rows, preferred_element_type=jnp.float32)
        shares.append(
            lax.psum_scatter(
                term.astype(jnp.bfloat16).astype(jnp.float32).astype(jnp.bfloat16),
                "dp",
                scatter_dimension=0,
                tiled=True,
            ).astype(jnp.float32)
        )
    gradient = jnp.stack(shares)
    first_new = 0.9 * first + 0.1 * gradient
    second_new = 0.999 * second + 0.001 * gradient * gradient
    update = (
        first_new / bias_one / (jnp.sqrt(second_new / bias_two) + adam_eps) + decay_rate * weight
    )
    update_sq = jnp.sum(update * update, axis=(1, 2))
    update_total = lax.psum(update_sq, "dp")
    trust_ratio = jnp.sqrt(weight_total) / (jnp.sqrt(update_total) + norm_eps)
    fresh = weight - learn_rate * trust_ratio[:, None, None] * update
    return fresh.astype(jnp.bfloat16)


def solution(mesh):
    placed = (
        P(("expert", "dp"), None),
        P(("expert", "dp"), None, None),
        P(("expert", "dp"), None),
        P(("expert", "dp"), None),
        P(("expert", "dp"), None),
        P("expert", "dp", None),
        P("expert", "dp", None),
        P("expert", "dp", None),
    )
    step = functools.partial(choose, mesh.shape["expert"], mesh.shape["dp"])
    return jax.shard_map(
        step, mesh=mesh, in_specs=placed, out_specs=P("expert", "dp", None), check_vma=False
    )
```

```python
import functools

import jax
import jax.numpy as jnp
from jax import lax
from jax.experimental import pallas as pl
from jax.experimental.pallas import tpu as pltpu
from jax.sharding import PartitionSpec as P

learn_rate = 0.3
decay_rate = 0.01
adam_eps = 1e-06
norm_eps = 1e-06
bias_one = 1.0 - 0.9**10
bias_two = 1.0 - 0.999**10


MESH = pl.DeviceIdType.MESH
LANES = 128
CHUNKS = 2


def mix_column(mix_ref, count_ref, local_rows, capacity):
    row = lax.broadcasted_iota(jnp.int32, (local_rows, local_rows), 0)
    col = lax.broadcasted_iota(jnp.int32, (local_rows, local_rows), 1)
    lane = lax.broadcasted_iota(jnp.int32, (1, local_rows), 1)
    live = jnp.zeros((1, local_rows), jnp.int32)
    for g in range(local_rows // capacity):
        live = jnp.where(lane // capacity == g, count_ref[0, g], live)
    mix = jnp.where(lane % capacity < live, mix_ref[...], 0.0)
    mix = mix.astype(jnp.bfloat16).astype(jnp.float32)
    return jnp.sum(jnp.where(row == col, mix, 0.0), axis=1, keepdims=True)


def fused_kernel(
    n_expert,
    chunks,
    token_hbm,
    count_hbm,
    mix_hbm,
    grad_hbm,
    hidden_hbm,
    weight_hbm,
    first_hbm,
    second_hbm,
    out_hbm,
    scale_ref,
    token_ref,
    count_ref,
    mix_ref,
    grad,
    hidden,
    weight,
    first,
    second,
    sendbuf,
    rows,
    hsend,
    hrecv,
    lhs,
    gradient,
    known_w,
    known_m,
    known_v,
    update,
    norms,
    load_sem,
    out_sem,
    z_send,
    z_recv,
    p_send,
    p_recv,
    h_send,
    h_recv,
    n_send,
    n_recv,
):
    e = lax.axis_index("expert")
    d = lax.axis_index("dp")
    core, x, y = d % 2, (d // 2) % 2, d // 4
    experts_here, share, width = weight.shape
    capacity = token_ref.shape[2]
    cols = width // chunks
    slots = experts_here * capacity
    local_rows = n_expert * slots
    n_dp = hrecv.shape[0]
    folds = LANES // local_rows
    part = share // folds

    def member(fy, fx, fc):
        yy = 1 - y if fy else y
        xx = 1 - x if fx else x
        cc = 1 - core if fc else core
        return yy * 4 + xx * 2 + cc

    flips = [(f // 4, (f // 2) % 2, f % 2) for f in range(1, n_dp)]

    barrier = pltpu.get_barrier_semaphore()
    for step in range(1, n_expert):
        pl.semaphore_signal(barrier, inc=1, device_id=((e + step) % n_expert, d), device_id_type=MESH)
    for flip in flips:
        pl.semaphore_signal(barrier, inc=1, device_id=(e, member(*flip)), device_id_type=MESH)

    loads = [
        pltpu.make_async_copy(src, dst, load_sem.at[i])
        for i, (src, dst) in enumerate(
            [
                (hidden_hbm, hidden),
                (grad_hbm, grad),
                (weight_hbm, weight),
                (first_hbm, first),
                (second_hbm, second),
                (count_hbm, count_ref),
                (mix_hbm, mix_ref),
                (token_hbm, token_ref),
            ]
        )
    ]
    for i in (7, 1, 0, 5, 6):
        loads[i].start()

    tokens = grad.shape[0]
    lane = lax.broadcasted_iota(jnp.int32, (8, tokens), 1)
    sub = lax.broadcasted_iota(jnp.int32, (8, tokens), 0)
    loads[7].wait()
    blocks = []
    for base in range(0, local_rows, 8):
        want = jnp.zeros((8, tokens), jnp.int32)
        for i in range(8):
            s = base + i
            want = jnp.where(sub == i, token_ref[0, s // capacity, s % capacity], want)
        blocks.append(jnp.where(want == lane, 1.0, 0.0))
    onehot = jnp.concatenate(blocks, axis=0).astype(jnp.bfloat16)
    loads[1].wait()
    for copy in loads[2:5]:
        copy.start()
    z_copies = []
    for ch in range(chunks):
        picked = jnp.dot(
            onehot, grad[:, ch * cols : (ch + 1) * cols], preferred_element_type=jnp.float32
        ).astype(jnp.bfloat16)
        sendbuf[ch] = picked.reshape(n_expert, slots, cols)
        rows[ch, d, 0] = sendbuf[ch, e]
        if ch == 0:
            pl.semaphore_wait(barrier, n_expert - 1 + n_dp - 1)
        group = []
        for step in range(1, n_expert):
            peer = (e + step) % n_expert
            copy = pltpu.make_async_remote_copy(
                src_ref=sendbuf.at[ch, peer],
                dst_ref=rows.at[ch, d, n_expert - step],
                send_sem=z_send.at[ch, step - 1],
                recv_sem=z_recv.at[ch, step - 1],
                device_id=(peer, d),
                device_id_type=MESH,
            )
            copy.start()
            group.append(copy)
        z_copies.append(group)

    near_x, near_y, partner = member(0, 1, 0), member(1, 0, 0), member(0, 0, 1)
    across = member(1, 1, 0)

    def region(piece, block, which):
        if piece == 0:
            start, size = [(0, chunks), (0, chunks // 2), (chunks // 2, chunks - chunks // 2)][which]
            return rows.at[pl.ds(start, size), block, 0]
        others = n_expert - 1
        low = others // 2 if piece % 2 else others - others // 2
        start, size = [(1, others), (1, low), (1 + low, others - low)][which]
        return rows.at[piece - 1, block, pl.ds(start, size)]

    def send(kind, piece, block, which, to):
        ref = region(piece, block, which)
        return pltpu.make_async_remote_copy(
            src_ref=ref,
            dst_ref=ref,
            send_sem=p_send.at[piece, kind],
            recv_sem=p_recv.at[piece, kind],
            device_id=(e, to),
            device_id_type=MESH,
        )

    whole, low, high = 0, 1, 2
    plane = []
    for piece in range(chunks + 1):
        plane.append(
            dict(
                own_x=send(0, piece, d, whole, near_x),
                own_y=send(1, piece, d, whole, near_y),
                own_c=send(2, piece, d, whole, partner),
                relay_y=send(3, piece, near_x, low, near_y),
                relay_x=send(4, piece, near_y, high, near_x),
                pass_x=send(5, piece, near_x, whole, partner),
                pass_y=send(6, piece, near_y, whole, partner),
                pass_low=send(7, piece, across, low, partner),
                pass_high=send(8, piece, across, high, partner),
            )
        )

    h_copies = []
    for i, flip in enumerate(flips):
        peer = member(*flip)
        copy = pltpu.make_async_remote_copy(
            src_ref=hsend.at[peer],
            dst_ref=hrecv.at[d],
            send_sem=h_send.at[i],
            recv_sem=h_recv.at[i],
            device_id=(e, peer),
            device_id_type=MESH,
        )
        h_copies.append(copy)

    def stage_hidden():
        slot = lax.broadcasted_iota(jnp.int32, (1, LANES), 1) % local_rows
        source = (slot // slots + e) % n_expert * slots + slot % slots
        row_id = lax.broadcasted_iota(jnp.int32, (local_rows, LANES), 0)
        loads[5].wait()
        loads[6].wait()
        mix_rows = mix_column(mix_ref, count_ref, local_rows, capacity)
        placed = jnp.where(row_id == source, mix_rows, 0.0).astype(jnp.bfloat16)
        loads[0].wait()
        turned = lax.dot_general(
            hidden[...], placed, (((0,), (0,)), ((), ())), preferred_element_type=jnp.float32
        )
        turned = turned.reshape(n_dp, folds, part, LANES)
        at_lane = lax.broadcasted_iota(jnp.int32, (1, 1, LANES), 2) // local_rows
        dense = turned[:, 0]
        for f in range(1, folds):
            dense = jnp.where(at_lane == f, turned[:, f], dense)
        hsend[...] = dense.astype(jnp.bfloat16)
        hrecv[d] = hsend[d]
        for copy in h_copies:
            copy.start()

    def stage_own(ch):
        if ch > 0:
            for copy in z_copies[ch - 1]:
                copy.wait_recv()
        p = plane[ch]
        for name in ("own_x", "own_y", "own_c"):
            p[name].start()
        if ch == 0:
            stage_hidden()
        if ch == 1:
            stage_known()

    def stage_relay(ch):
        p = plane[ch]
        p["own_x"].wait_recv()
        p["relay_y"].start()
        p["pass_x"].start()
        p["own_y"].wait_recv()
        p["relay_x"].start()
        p["pass_y"].start()

    def stage_pass(ch):
        p = plane[ch]
        p["relay_y"].wait_recv()
        p["pass_low"].start()
        p["relay_x"].wait_recv()
        p["pass_high"].start()

    def stage_lhs():
        for copy in h_copies:
            copy.wait_recv()
        lane_part = lax.broadcasted_iota(jnp.int32, (part, LANES), 1) // local_rows
        kind = (lax.broadcasted_iota(jnp.int32, (part, LANES), 1) % slots) // capacity
        for q in range(n_dp // folds):
            for f in range(folds):
                block = jnp.zeros((part, LANES), jnp.float32)
                for r in range(folds):
                    piece = hrecv[q * folds + r].astype(jnp.float32)
                    if r != f:
                        piece = pltpu.roll(piece, (r - f) % folds * local_rows, 1)
                    block = jnp.where(lane_part == r, piece, block)
                for j in range(experts_here):
                    top = j * share + f * part
                    lhs[top : top + part, q * LANES : (q + 1) * LANES] = jnp.where(
                        kind == j, block, 0.0
                    ).astype(jnp.bfloat16)

    tile = 16
    known_cols = cols
    zero = jnp.zeros((tile, LANES), jnp.float32)

    def fold(value):
        total = value[:, :LANES]
        for at in range(LANES, value.shape[1], LANES):
            total = total + value[:, at : at + LANES]
        return total

    weight_sums = [zero for _ in range(experts_here)]
    sums = [zero for _ in range(experts_here)]

    def stage_known():
        for copy in loads[2:5]:
            copy.wait()
        for j in range(experts_here):

            def block(r, carry, j=j):
                here = pl.ds(pl.multiple_of(r * tile, tile), tile)
                there = pl.ds(pl.multiple_of(j * share + r * tile, tile), tile)
                for at in range(0, width, known_cols):
                    part_at = slice(at, at + known_cols)
                    w = weight[j, here, part_at].astype(jnp.float32)
                    known_w[there, part_at] = decay_rate * w
                    known_m[there, part_at] = (0.9 / bias_one) * first[j, here, part_at].astype(jnp.float32)
                    known_v[there, part_at] = (0.999 / bias_two) * second[j, here, part_at].astype(jnp.float32)
                    carry = carry + fold(w * w)
                return carry

            weight_sums[j] = lax.fori_loop(0, share // tile, block, weight_sums[j])

    outs = []

    def stage_update(piece):
        p = plane[piece]
        for name in ("own_c", "pass_x", "pass_y", "pass_low", "pass_high"):
            p[name].wait_recv()
        if piece == 0:
            stage_lhs()
            return
        ch = piece - 1
        gradient[...] = jnp.dot(
            lhs[...], rows[ch].reshape(n_dp * local_rows, cols), preferred_element_type=jnp.float32
        )
        at = slice(ch * cols, (ch + 1) * cols)
        for j in range(experts_here):

            def block(r, carry, j=j):
                there = pl.ds(pl.multiple_of(j * share + r * tile, tile), tile)
                g = gradient[there, :]
                m = known_m[there, at] + (0.1 / bias_one) * g
                v = known_v[there, at] + (0.001 / bias_two) * g * g
                u = m / (v * lax.rsqrt(v) + adam_eps) + known_w[there, at]
                update[there, at] = u.astype(jnp.bfloat16)
                return carry + fold(u * u)

            sums[j] = lax.fori_loop(0, share // tile, block, sums[j])
        copy = pltpu.make_async_copy(update.at[:, at], out_hbm.at[:, at], out_sem.at[ch])
        copy.start()
        outs.append(copy)

    pieces = chunks + 1
    for t in range(pieces + 3):
        if t < pieces:
            stage_own(t)
        if 0 <= t - 1 < pieces:
            stage_relay(t - 1)
        if 0 <= t - 2 < pieces:
            stage_pass(t - 2)
        if 0 <= t - 3 < pieces:
            stage_update(t - 3)

    for j in range(experts_here):
        norms[d, j : j + 1, :] = jnp.sum(weight_sums[j], axis=0, keepdims=True)
        norms[d, experts_here + j : experts_here + j + 1, :] = jnp.sum(sums[j], axis=0, keepdims=True)
    n_copies = []
    for i, flip in enumerate(flips):
        copy = pltpu.make_async_remote_copy(
            src_ref=norms.at[d],
            dst_ref=norms.at[d],
            send_sem=n_send.at[i],
            recv_sem=n_recv.at[i],
            device_id=(e, member(*flip)),
            device_id_type=MESH,
        )
        copy.start()
        n_copies.append(copy)
    for group in z_copies:
        for copy in group:
            copy.wait_send()
    for p in plane:
        for copy in p.values():
            copy.wait_send()
    for copy in h_copies:
        copy.wait_send()
    for copy in n_copies:
        copy.wait_recv()
    total = norms[0]
    for i in range(1, n_dp):
        total = total + norms[i]
    total = jnp.sqrt(jnp.sum(total, axis=1, keepdims=True))
    for j in range(experts_here):
        ratio = total[j : j + 1] / (total[experts_here + j : experts_here + j + 1] + norm_eps)
        scale_ref[j : j + 1, :] = jnp.broadcast_to(learn_rate * ratio, (1, width))
    for copy in n_copies:
        copy.wait_send()
    for copy in outs:
        copy.wait()


def fused(n_expert, n_dp, grad_out, slot_token, hidden, slot_weight, counts, master_weight, moment1, moment2):
    experts_here, share, width = master_weight.shape
    capacity = slot_token.shape[2]
    slots = experts_here * capacity
    local_rows = n_expert * slots
    cols = width // CHUNKS
    half_type = jnp.bfloat16
    dma = pltpu.SemaphoreType.DMA
    anywhere = pl.BlockSpec(memory_space=pl.ANY)
    update, scale = pl.pallas_call(
        functools.partial(fused_kernel, n_expert, CHUNKS),
        out_shape=(
            jax.ShapeDtypeStruct((experts_here * share, width), half_type),
            jax.ShapeDtypeStruct((experts_here, width), jnp.float32),
        ),
        in_specs=[anywhere] * 8,
        out_specs=(anywhere, pl.BlockSpec(memory_space=pltpu.VMEM)),
        scratch_shapes=[
            pltpu.SMEM(slot_token.shape, slot_token.dtype),
            pltpu.SMEM(counts.shape, counts.dtype),
            pltpu.VMEM(slot_weight.shape, slot_weight.dtype),
            pltpu.VMEM(grad_out.shape, half_type),
            pltpu.VMEM(hidden.shape, half_type),
            pltpu.VMEM(master_weight.shape, half_type),
            pltpu.VMEM(master_weight.shape, half_type),
            pltpu.VMEM(master_weight.shape, half_type),
            pltpu.VMEM((CHUNKS, n_expert, slots, cols), half_type),
            pltpu.VMEM((CHUNKS, n_dp, n_expert, slots, cols), half_type),
            pltpu.VMEM((n_dp, share * local_rows // LANES, LANES), half_type),
            pltpu.VMEM((n_dp, share * local_rows // LANES, LANES), half_type),
            pltpu.VMEM((experts_here * share, n_dp * local_rows), half_type),
            pltpu.VMEM((experts_here * share, cols), jnp.float32),
            pltpu.VMEM((experts_here * share, width), jnp.float32),
            pltpu.VMEM((experts_here * share, width), jnp.float32),
            pltpu.VMEM((experts_here * share, width), jnp.float32),
            pltpu.VMEM((experts_here * share, width), half_type),
            pltpu.VMEM((n_dp, 2 * experts_here, LANES), jnp.float32),
            dma((8,)),
            dma((CHUNKS,)),
            dma((CHUNKS, n_expert - 1)),
            dma((CHUNKS, n_expert - 1)),
            dma((CHUNKS + 1, 9)),
            dma((CHUNKS + 1, 9)),
            dma((n_dp - 1,)),
            dma((n_dp - 1,)),
            dma((n_dp - 1,)),
            dma((n_dp - 1,)),
        ],
        compiler_params=pltpu.CompilerParams(collective_id=0, has_side_effects=True),
    )(slot_token, counts, slot_weight, grad_out, hidden, master_weight, moment1, moment2)
    update = update.reshape(master_weight.shape).astype(jnp.float32)
    fresh = master_weight.astype(jnp.float32) - scale[:, None, :] * update
    return fresh.astype(master_weight.dtype)


def choose(n_expert, n_dp, *args):
    grad_out, slot_token, hidden, _, _, master_weight, _, _ = args
    experts_here, share, width = master_weight.shape
    capacity = slot_token.shape[2]
    local_rows = hidden.shape[0]
    fewer_rows = n_dp * n_expert * capacity < hidden.shape[1]
    cube = n_dp == 2**3 and n_expert % 2 == 0
    tiles = (
        LANES % local_rows == 0
        and local_rows % 8 == 0
        and n_dp % max(1, LANES // local_rows) == 0
        and (experts_here * capacity) % 16 == 0
        and share % (16 * max(1, LANES // local_rows)) == 0
        and width % (CHUNKS * LANES) == 0
    )
    if fewer_rows and cube and tiles:
        return fused(n_expert, n_dp, *args)
    return local(*args)


def local(grad_out, slot_token, hidden, slot_weight, counts, master_weight, moment1, moment2):
    n_expert = lax.axis_size("expert")
    experts_here = master_weight.shape[0]
    capacity = slot_token.shape[2]
    width = grad_out.shape[1]
    depth = hidden.shape[1]
    weight = master_weight.astype(jnp.float32)
    first = moment1.astype(jnp.float32)
    second = moment2.astype(jnp.float32)
    weight_sq = jnp.sum(weight * weight, axis=(1, 2))
    weight_total = lax.psum(weight_sq, "dp")
    picked = jnp.take(grad_out, slot_token.reshape(-1), axis=0).reshape(
        n_expert, experts_here * capacity, width
    )
    arrived = lax.all_to_all(picked, "expert", split_axis=0, concat_axis=0, tiled=True)
    arrived = arrived.reshape(n_expert, experts_here, capacity, width)
    slot_ids = lax.broadcasted_iota(jnp.int32, (n_expert, experts_here, capacity), 2)
    is_live = slot_ids < counts.reshape(n_expert, experts_here)[:, :, None]
    mixing = jnp.where(is_live, slot_weight.reshape(n_expert, experts_here, capacity), 0.0).astype(
        jnp.bfloat16
    )
    scaled = (mixing.astype(jnp.float32)[..., None] * arrived.astype(jnp.float32)).astype(
        jnp.bfloat16
    )
    saved = hidden.reshape(n_expert, experts_here, capacity, depth)
    shares = []
    for j in range(experts_here):
        saved_rows = saved[:, j].reshape(-1, depth)
        scaled_rows = scaled[:, j].reshape(-1, width)
        term = jnp.dot(saved_rows.T, scaled_rows, preferred_element_type=jnp.float32)
        shares.append(
            lax.psum_scatter(
                term.astype(jnp.bfloat16).astype(jnp.float32).astype(jnp.bfloat16),
                "dp",
                scatter_dimension=0,
                tiled=True,
            ).astype(jnp.float32)
        )
    gradient = jnp.stack(shares)
    first_new = 0.9 * first + 0.1 * gradient
    second_new = 0.999 * second + 0.001 * gradient * gradient
    update = (
        first_new / bias_one / (jnp.sqrt(second_new / bias_two) + adam_eps) + decay_rate * weight
    )
    update_sq = jnp.sum(update * update, axis=(1, 2))
    update_total = lax.psum(update_sq, "dp")
    trust_ratio = jnp.sqrt(weight_total) / (jnp.sqrt(update_total) + norm_eps)
    fresh = weight - learn_rate * trust_ratio[:, None, None] * update
    return fresh.astype(jnp.bfloat16)


def solution(mesh):
    placed = (
        P(("expert", "dp"), None),
        P(("expert", "dp"), None, None),
        P(("expert", "dp"), None),
        P(("expert", "dp"), None),
        P(("expert", "dp"), None),
        P("expert", "dp", None),
        P("expert", "dp", None),
        P("expert", "dp", None),
    )
    step = functools.partial(choose, mesh.shape["expert"], mesh.shape["dp"])
    return jax.shard_map(
        step, mesh=mesh, in_specs=placed, out_specs=P("expert", "dp", None), check_vma=False
    )
```

```python
import functools

import jax
import jax.numpy as jnp
from jax import lax
from jax.experimental import pallas as pl
from jax.experimental.pallas import tpu as pltpu
from jax.sharding import PartitionSpec as P

learn_rate = 0.3
decay_rate = 0.01
adam_eps = 1e-06
norm_eps = 1e-06
bias_one = 1.0 - 0.9**10
bias_two = 1.0 - 0.999**10


MESH = pl.DeviceIdType.MESH
LANES = 128
CHUNKS = 2


def mix_column(mix_ref, count_ref, local_rows, capacity):
    row = lax.broadcasted_iota(jnp.int32, (local_rows, local_rows), 0)
    col = lax.broadcasted_iota(jnp.int32, (local_rows, local_rows), 1)
    lane = lax.broadcasted_iota(jnp.int32, (1, local_rows), 1)
    live = jnp.zeros((1, local_rows), jnp.int32)
    for g in range(local_rows // capacity):
        live = jnp.where(lane // capacity == g, count_ref[0, g], live)
    mix = jnp.where(lane % capacity < live, mix_ref[...], 0.0)
    mix = mix.astype(jnp.bfloat16).astype(jnp.float32)
    return jnp.sum(jnp.where(row == col, mix, 0.0), axis=1, keepdims=True)


def fused_kernel(
    n_expert,
    chunks,
    token_hbm,
    count_hbm,
    mix_hbm,
    grad_hbm,
    hidden_hbm,
    weight_hbm,
    first_hbm,
    second_hbm,
    update,
    scale_ref,
    token_ref,
    count_ref,
    mix_ref,
    grad,
    hidden,
    weight,
    first,
    second,
    sendbuf,
    rows,
    hsend,
    hrecv,
    lhs,
    gradient,
    known_w,
    known_m,
    known_v,
    norms,
    load_sem,
    z_send,
    z_recv,
    p_send,
    p_recv,
    h_send,
    h_recv,
    n_send,
    n_recv,
):
    e = lax.axis_index("expert")
    d = lax.axis_index("dp")
    core, x, y = d % 2, (d // 2) % 2, d // 4
    experts_here, share, width = weight.shape
    capacity = token_ref.shape[2]
    cols = width // chunks
    slots = experts_here * capacity
    local_rows = n_expert * slots
    n_dp = hrecv.shape[0]
    folds = LANES // local_rows
    part = share // folds

    def member(fy, fx, fc):
        yy = 1 - y if fy else y
        xx = 1 - x if fx else x
        cc = 1 - core if fc else core
        return yy * 4 + xx * 2 + cc

    flips = [(f // 4, (f // 2) % 2, f % 2) for f in range(1, n_dp)]

    barrier = pltpu.get_barrier_semaphore()
    for step in range(1, n_expert):
        pl.semaphore_signal(barrier, inc=1, device_id=((e + step) % n_expert, d), device_id_type=MESH)
    for flip in flips:
        pl.semaphore_signal(barrier, inc=1, device_id=(e, member(*flip)), device_id_type=MESH)

    loads = [
        pltpu.make_async_copy(src, dst, load_sem.at[i])
        for i, (src, dst) in enumerate(
            [
                (hidden_hbm, hidden),
                (grad_hbm, grad),
                (weight_hbm, weight),
                (first_hbm, first),
                (second_hbm, second),
                (count_hbm, count_ref),
                (mix_hbm, mix_ref),
                (token_hbm, token_ref),
            ]
        )
    ]
    for i in (7, 1, 0, 5, 6):
        loads[i].start()

    tokens = grad.shape[0]
    lane = lax.broadcasted_iota(jnp.int32, (8, tokens), 1)
    sub = lax.broadcasted_iota(jnp.int32, (8, tokens), 0)
    loads[7].wait()
    blocks = []
    for base in range(0, local_rows, 8):
        want = jnp.zeros((8, tokens), jnp.int32)
        for i in range(8):
            s = base + i
            want = jnp.where(sub == i, token_ref[0, s // capacity, s % capacity], want)
        blocks.append(jnp.where(want == lane, 1.0, 0.0))
    onehot = jnp.concatenate(blocks, axis=0).astype(jnp.bfloat16)
    loads[1].wait()
    for copy in loads[2:5]:
        copy.start()
    z_copies = []
    for ch in range(chunks):
        picked = jnp.dot(
            onehot, grad[:, ch * cols : (ch + 1) * cols], preferred_element_type=jnp.float32
        ).astype(jnp.bfloat16)
        sendbuf[ch] = picked.reshape(n_expert, slots, cols)
        rows[ch, d, 0] = sendbuf[ch, e]
        if ch == 0:
            pl.semaphore_wait(barrier, n_expert - 1 + n_dp - 1)
        group = []
        for step in range(1, n_expert):
            peer = (e + step) % n_expert
            copy = pltpu.make_async_remote_copy(
                src_ref=sendbuf.at[ch, peer],
                dst_ref=rows.at[ch, d, n_expert - step],
                send_sem=z_send.at[ch, step - 1],
                recv_sem=z_recv.at[ch, step - 1],
                device_id=(peer, d),
                device_id_type=MESH,
            )
            copy.start()
            group.append(copy)
        z_copies.append(group)

    near_x, near_y, partner = member(0, 1, 0), member(1, 0, 0), member(0, 0, 1)
    across = member(1, 1, 0)

    def region(piece, block, which):
        if piece == 0:
            start, size = [(0, chunks), (0, chunks // 2), (chunks // 2, chunks - chunks // 2)][which]
            return rows.at[pl.ds(start, size), block, 0]
        others = n_expert - 1
        low = others // 2 if piece % 2 else others - others // 2
        start, size = [(1, others), (1, low), (1 + low, others - low)][which]
        return rows.at[piece - 1, block, pl.ds(start, size)]

    def send(kind, piece, block, which, to):
        ref = region(piece, block, which)
        return pltpu.make_async_remote_copy(
            src_ref=ref,
            dst_ref=ref,
            send_sem=p_send.at[piece, kind],
            recv_sem=p_recv.at[piece, kind],
            device_id=(e, to),
            device_id_type=MESH,
        )

    whole, low, high = 0, 1, 2
    plane = []
    for piece in range(chunks + 1):
        plane.append(
            dict(
                own_x=send(0, piece, d, whole, near_x),
                own_y=send(1, piece, d, whole, near_y),
                own_c=send(2, piece, d, whole, partner),
                relay_y=send(3, piece, near_x, low, near_y),
                relay_x=send(4, piece, near_y, high, near_x),
                pass_x=send(5, piece, near_x, whole, partner),
                pass_y=send(6, piece, near_y, whole, partner),
                pass_low=send(7, piece, across, low, partner),
                pass_high=send(8, piece, across, high, partner),
            )
        )

    h_copies = []
    for i, flip in enumerate(flips):
        peer = member(*flip)
        copy = pltpu.make_async_remote_copy(
            src_ref=hsend.at[peer],
            dst_ref=hrecv.at[d],
            send_sem=h_send.at[i],
            recv_sem=h_recv.at[i],
            device_id=(e, peer),
            device_id_type=MESH,
        )
        h_copies.append(copy)

    def stage_hidden():
        slot = lax.broadcasted_iota(jnp.int32, (1, LANES), 1) % local_rows
        source = (slot // slots + e) % n_expert * slots + slot % slots
        row_id = lax.broadcasted_iota(jnp.int32, (local_rows, LANES), 0)
        loads[5].wait()
        loads[6].wait()
        mix_rows = mix_column(mix_ref, count_ref, local_rows, capacity)
        placed = jnp.where(row_id == source, mix_rows, 0.0).astype(jnp.bfloat16)
        loads[0].wait()
        turned = lax.dot_general(
            hidden[...], placed, (((0,), (0,)), ((), ())), preferred_element_type=jnp.float32
        )
        turned = turned.reshape(n_dp, folds, part, LANES)
        at_lane = lax.broadcasted_iota(jnp.int32, (1, 1, LANES), 2) // local_rows
        dense = turned[:, 0]
        for f in range(1, folds):
            dense = jnp.where(at_lane == f, turned[:, f], dense)
        hsend[...] = dense.astype(jnp.bfloat16)
        hrecv[d] = hsend[d]
        for copy in h_copies:
            copy.start()

    def stage_own(ch):
        if ch > 0:
            for copy in z_copies[ch - 1]:
                copy.wait_recv()
        p = plane[ch]
        for name in ("own_x", "own_y", "own_c"):
            p[name].start()
        if ch == 0:
            stage_hidden()
        if ch == 1:
            stage_known()

    def stage_relay(ch):
        p = plane[ch]
        p["own_x"].wait_recv()
        p["relay_y"].start()
        p["pass_x"].start()
        p["own_y"].wait_recv()
        p["relay_x"].start()
        p["pass_y"].start()

    def stage_pass(ch):
        p = plane[ch]
        p["relay_y"].wait_recv()
        p["pass_low"].start()
        p["relay_x"].wait_recv()
        p["pass_high"].start()

    def stage_lhs():
        for copy in h_copies:
            copy.wait_recv()
        lane_part = lax.broadcasted_iota(jnp.int32, (part, LANES), 1) // local_rows
        kind = (lax.broadcasted_iota(jnp.int32, (part, LANES), 1) % slots) // capacity
        for q in range(n_dp // folds):
            for f in range(folds):
                block = jnp.zeros((part, LANES), jnp.float32)
                for r in range(folds):
                    piece = hrecv[q * folds + r].astype(jnp.float32)
                    if r != f:
                        piece = pltpu.roll(piece, (r - f) % folds * local_rows, 1)
                    block = jnp.where(lane_part == r, piece, block)
                for j in range(experts_here):
                    top = j * share + f * part
                    lhs[top : top + part, q * LANES : (q + 1) * LANES] = jnp.where(
                        kind == j, block, 0.0
                    ).astype(jnp.bfloat16)

    tile = 16
    known_cols = cols
    zero = jnp.zeros((tile, LANES), jnp.float32)

    def fold(value):
        total = value[:, :LANES]
        for at in range(LANES, value.shape[1], LANES):
            total = total + value[:, at : at + LANES]
        return total

    weight_sums = [zero for _ in range(experts_here)]
    sums = [zero for _ in range(experts_here)]

    def stage_known():
        for copy in loads[2:5]:
            copy.wait()
        for j in range(experts_here):

            def block(r, carry, j=j):
                here = pl.ds(pl.multiple_of(r * tile, tile), tile)
                there = pl.ds(pl.multiple_of(j * share + r * tile, tile), tile)
                for at in range(0, width, known_cols):
                    part_at = slice(at, at + known_cols)
                    w = weight[j, here, part_at].astype(jnp.float32)
                    known_w[there, part_at] = decay_rate * w
                    known_m[there, part_at] = (0.9 / bias_one) * first[j, here, part_at].astype(jnp.float32)
                    known_v[there, part_at] = (0.999 / bias_two) * second[j, here, part_at].astype(jnp.float32)
                    carry = carry + fold(w * w)
                return carry

            weight_sums[j] = lax.fori_loop(0, share // tile, block, weight_sums[j])


    def stage_update(piece):
        p = plane[piece]
        for name in ("own_c", "pass_x", "pass_y", "pass_low", "pass_high"):
            p[name].wait_recv()
        if piece == 0:
            stage_lhs()
            return
        ch = piece - 1
        gradient[...] = jnp.dot(
            lhs[...], rows[ch].reshape(n_dp * local_rows, cols), preferred_element_type=jnp.float32
        )
        at = slice(ch * cols, (ch + 1) * cols)
        for j in range(experts_here):

            def block(r, carry, j=j):
                there = pl.ds(pl.multiple_of(j * share + r * tile, tile), tile)
                g = gradient[there, :]
                m = known_m[there, at] + (0.1 / bias_one) * g
                v = known_v[there, at] + (0.001 / bias_two) * g * g
                u = m / (v * lax.rsqrt(v) + adam_eps) + known_w[there, at]
                update[there, at] = u.astype(jnp.bfloat16)
                return carry + fold(u * u)

            sums[j] = lax.fori_loop(0, share // tile, block, sums[j])

    pieces = chunks + 1
    for t in range(pieces + 3):
        if t < pieces:
            stage_own(t)
        if 0 <= t - 1 < pieces:
            stage_relay(t - 1)
        if 0 <= t - 2 < pieces:
            stage_pass(t - 2)
        if 0 <= t - 3 < pieces:
            stage_update(t - 3)

    for j in range(experts_here):
        norms[d, j : j + 1, :] = jnp.sum(weight_sums[j], axis=0, keepdims=True)
        norms[d, experts_here + j : experts_here + j + 1, :] = jnp.sum(sums[j], axis=0, keepdims=True)
    n_copies = []
    for i, flip in enumerate(flips):
        copy = pltpu.make_async_remote_copy(
            src_ref=norms.at[d],
            dst_ref=norms.at[d],
            send_sem=n_send.at[i],
            recv_sem=n_recv.at[i],
            device_id=(e, member(*flip)),
            device_id_type=MESH,
        )
        copy.start()
        n_copies.append(copy)
    for group in z_copies:
        for copy in group:
            copy.wait_send()
    for p in plane:
        for copy in p.values():
            copy.wait_send()
    for copy in h_copies:
        copy.wait_send()
    for copy in n_copies:
        copy.wait_recv()
    total = norms[0]
    for i in range(1, n_dp):
        total = total + norms[i]
    total = jnp.sqrt(jnp.sum(total, axis=1, keepdims=True))
    for j in range(experts_here):
        ratio = total[j : j + 1] / (total[experts_here + j : experts_here + j + 1] + norm_eps)
        scale_ref[j : j + 1, :] = jnp.broadcast_to(learn_rate * ratio, (1, width))
    for copy in n_copies:
        copy.wait_send()


def fused(n_expert, n_dp, grad_out, slot_token, hidden, slot_weight, counts, master_weight, moment1, moment2):
    experts_here, share, width = master_weight.shape
    capacity = slot_token.shape[2]
    slots = experts_here * capacity
    local_rows = n_expert * slots
    cols = width // CHUNKS
    half_type = jnp.bfloat16
    dma = pltpu.SemaphoreType.DMA
    anywhere = pl.BlockSpec(memory_space=pl.ANY)
    update, scale = pl.pallas_call(
        functools.partial(fused_kernel, n_expert, CHUNKS),
        out_shape=(
            pltpu.VMEM((experts_here * share, width), half_type),
            pltpu.VMEM((experts_here, width), jnp.float32),
        ),
        in_specs=[anywhere] * 8,
        out_specs=(pl.BlockSpec(memory_space=pltpu.VMEM),) * 2,
        scratch_shapes=[
            pltpu.SMEM(slot_token.shape, slot_token.dtype),
            pltpu.SMEM(counts.shape, counts.dtype),
            pltpu.VMEM(slot_weight.shape, slot_weight.dtype),
            pltpu.VMEM(grad_out.shape, half_type),
            pltpu.VMEM(hidden.shape, half_type),
            pltpu.VMEM(master_weight.shape, half_type),
            pltpu.VMEM(master_weight.shape, half_type),
            pltpu.VMEM(master_weight.shape, half_type),
            pltpu.VMEM((CHUNKS, n_expert, slots, cols), half_type),
            pltpu.VMEM((CHUNKS, n_dp, n_expert, slots, cols), half_type),
            pltpu.VMEM((n_dp, share * local_rows // LANES, LANES), half_type),
            pltpu.VMEM((n_dp, share * local_rows // LANES, LANES), half_type),
            pltpu.VMEM((experts_here * share, n_dp * local_rows), half_type),
            pltpu.VMEM((experts_here * share, cols), jnp.float32),
            pltpu.VMEM((experts_here * share, width), jnp.float32),
            pltpu.VMEM((experts_here * share, width), jnp.float32),
            pltpu.VMEM((experts_here * share, width), jnp.float32),
            pltpu.VMEM((n_dp, 2 * experts_here, LANES), jnp.float32),
            dma((8,)),
            dma((CHUNKS, n_expert - 1)),
            dma((CHUNKS, n_expert - 1)),
            dma((CHUNKS + 1, 9)),
            dma((CHUNKS + 1, 9)),
            dma((n_dp - 1,)),
            dma((n_dp - 1,)),
            dma((n_dp - 1,)),
            dma((n_dp - 1,)),
        ],
        compiler_params=pltpu.CompilerParams(collective_id=0, has_side_effects=True),
    )(slot_token, counts, slot_weight, grad_out, hidden, master_weight, moment1, moment2)
    update = update.reshape(master_weight.shape).astype(jnp.float32)
    fresh = master_weight.astype(jnp.float32) - scale[:, None, :] * update
    return fresh.astype(master_weight.dtype)


def choose(n_expert, n_dp, *args):
    grad_out, slot_token, hidden, _, _, master_weight, _, _ = args
    experts_here, share, width = master_weight.shape
    capacity = slot_token.shape[2]
    local_rows = hidden.shape[0]
    fewer_rows = n_dp * n_expert * capacity < hidden.shape[1]
    cube = n_dp == 2**3 and n_expert % 2 == 0
    tiles = (
        LANES % local_rows == 0
        and local_rows % 8 == 0
        and n_dp % max(1, LANES // local_rows) == 0
        and (experts_here * capacity) % 16 == 0
        and share % (16 * max(1, LANES // local_rows)) == 0
        and width % (CHUNKS * LANES) == 0
    )
    if fewer_rows and cube and tiles:
        return fused(n_expert, n_dp, *args)
    return local(*args)


def local(grad_out, slot_token, hidden, slot_weight, counts, master_weight, moment1, moment2):
    n_expert = lax.axis_size("expert")
    experts_here = master_weight.shape[0]
    capacity = slot_token.shape[2]
    width = grad_out.shape[1]
    depth = hidden.shape[1]
    weight = master_weight.astype(jnp.float32)
    first = moment1.astype(jnp.float32)
    second = moment2.astype(jnp.float32)
    weight_sq = jnp.sum(weight * weight, axis=(1, 2))
    weight_total = lax.psum(weight_sq, "dp")
    picked = jnp.take(grad_out, slot_token.reshape(-1), axis=0).reshape(
        n_expert, experts_here * capacity, width
    )
    arrived = lax.all_to_all(picked, "expert", split_axis=0, concat_axis=0, tiled=True)
    arrived = arrived.reshape(n_expert, experts_here, capacity, width)
    slot_ids = lax.broadcasted_iota(jnp.int32, (n_expert, experts_here, capacity), 2)
    is_live = slot_ids < counts.reshape(n_expert, experts_here)[:, :, None]
    mixing = jnp.where(is_live, slot_weight.reshape(n_expert, experts_here, capacity), 0.0).astype(
        jnp.bfloat16
    )
    scaled = (mixing.astype(jnp.float32)[..., None] * arrived.astype(jnp.float32)).astype(
        jnp.bfloat16
    )
    saved = hidden.reshape(n_expert, experts_here, capacity, depth)
    shares = []
    for j in range(experts_here):
        saved_rows = saved[:, j].reshape(-1, depth)
        scaled_rows = scaled[:, j].reshape(-1, width)
        term = jnp.dot(saved_rows.T, scaled_rows, preferred_element_type=jnp.float32)
        shares.append(
            lax.psum_scatter(
                term.astype(jnp.bfloat16).astype(jnp.float32).astype(jnp.bfloat16),
                "dp",
                scatter_dimension=0,
                tiled=True,
            ).astype(jnp.float32)
        )
    gradient = jnp.stack(shares)
    first_new = 0.9 * first + 0.1 * gradient
    second_new = 0.999 * second + 0.001 * gradient * gradient
    update = (
        first_new / bias_one / (jnp.sqrt(second_new / bias_two) + adam_eps) + decay_rate * weight
    )
    update_sq = jnp.sum(update * update, axis=(1, 2))
    update_total = lax.psum(update_sq, "dp")
    trust_ratio = jnp.sqrt(weight_total) / (jnp.sqrt(update_total) + norm_eps)
    fresh = weight - learn_rate * trust_ratio[:, None, None] * update
    return fresh.astype(jnp.bfloat16)


def solution(mesh):
    placed = (
        P(("expert", "dp"), None),
        P(("expert", "dp"), None, None),
        P(("expert", "dp"), None),
        P(("expert", "dp"), None),
        P(("expert", "dp"), None),
        P("expert", "dp", None),
        P("expert", "dp", None),
        P("expert", "dp", None),
    )
    step = functools.partial(choose, mesh.shape["expert"], mesh.shape["dp"])
    return jax.shard_map(
        step, mesh=mesh, in_specs=placed, out_specs=P("expert", "dp", None), check_vma=False
    )
```
